128 devices in a mesh: table: 8 (over x, core), row: 16 (over z, y).
Axes of the slice: x: 4, y: 4, z: 4, core: 2. Of those that a mesh axis runs over, the one named last changes fastest.
Arguments:
- features: bfloat16 [8192, 8192], P('row', 'table'), may hold values from -6 to 6
- cotangent: bfloat16 [8192, 8192], P('row', 'table'), may hold values from -6 to 6
- cross_in: bfloat16 [8192, 512], P('table'), may hold values from -0.0625 to 0.0625
- cross_out: bfloat16 [8192, 512], P('table'), may hold values from -0.25 to 0.25
- bias: float32 [8192], P('table'), may hold values from -6 to 6
- dest_shard: int32 [64, 8192, 1], P('table', 'row'), may hold values from 0 to 15; in each aligned block of 512 rows (0 to 511, 512 to 1023, ..., all dimensions but the last counted through in order) at most 48 rows name the same one
- quot_row: int32 [64, 8192], P('table', 'row'), may hold values from 0 to 1023
- rem_row: int32 [64, 8192], P('table', 'row'), may hold values from 0 to 2047
- quot_slab: bfloat16 [64, 16384, 128], P('table', 'row'), may hold values from -6 to 6
- quot_accum: float32 [64, 16384], P('table', 'row'), may hold values from 0.05 to 2
- rem_table: bfloat16 [64, 2048, 128], P('table'), may hold values from -6 to 6
- rem_accum: float32 [64, 2048], P('table'), may hold values from 0.5 to 20
Outputs:
- quot_out: bfloat16 [64, 16384, 128], P('table', 'row')
- quot_acc_out: float32 [64, 16384], P('table', 'row')
- rem_out: bfloat16 [64, 2048, 128], P('table')
- rem_acc_out: float32 [64, 2048], P('table', 'row')
The draws below stay inside these ranges and needn't reach their ends.
Inputs may be any that keep to these rules, and one draw needn't show every extreme that they name: `dest_shard`: for each table, the 512 samples of one index of row name one row shard at most 48 times, a bound that some block reaches.
All inputs are finite; a program needn't handle non-finite values.
Results may differ from the reference program's by a relative error of at most 0.004.
Values may be sent and summed in bfloat16 or wider, within the bound.
No kernel may reach another device: no remote copies, remote signals or barrier semaphores. Data moves between devices by JAX's collectives and lax.ppermute only.
A program may use at most 128 MiB of HBM per device.

```python
import math
import jax
import jax.numpy as jnp
import numpy as np
from jax import lax

EMB = 128
RANK = 512
REM = 2048
QR_DEV = 1024
B_DEV = 512
TABLES = 64
D = 8192
B = 8192
QROWS = 16384
CAP = 48
N_ROW = 16


def place_ends(drawn, rng, smallest, top_value):
    longest = drawn.shape.index(max(drawn.shape))
    spots = []
    for shift in (0, 1):
        where = [jax.random.randint(jax.random.fold_in(rng, axis), (), 0, length) for axis, length in enumerate(drawn.shape)]
        where[longest] = (where[longest] + shift) % drawn.shape[longest]
        spots.append(tuple(where))
    return drawn.at[spots[0]].set(smallest).at[spots[1]].set(top_value)


def shard_levels(rng, extent, pieces, least, top_value):
    def one(dim, shards_of):
        steps = jax.random.uniform(jax.random.fold_in(jax.random.fold_in(rng, 6), dim), (shards_of,), jnp.float32, least / len(pieces), top_value / len(pieces))
        return jnp.repeat(jnp.exp(steps), extent[dim] // shards_of).reshape((-1,) + (1,) * (len(extent) - dim - 1))

    gain = one(*pieces[0])
    for cut in pieces[1:]:
        gain = gain * one(*cut)
    return gain


def deal_out(stream_key, own, number, rows, number_of, top, limit, skew):
    sequence = jax.random.permutation(stream_key, number_of)
    heavy_load, usual = shares(number_of, rows * top, limit, skew, True), shares(number_of, rows * top, limit, skew, False)
    places = jnp.arange(number_of)

    def named(sizes, offset_by):
        used = int((sizes > 0).sum())
        fixed = max(1, used // 4)
        moved = fixed + (places - fixed + offset_by * (used - fixed)) % max(1, number_of - fixed)
        return jnp.zeros((number_of,), jnp.int32).at[sequence[jnp.where(places < fixed, places, moved)]].set(jnp.asarray(sizes, jnp.int32))

    sizes = jnp.where(number % 4 == 0, named(heavy_load, number // 4), named(usual, number - number // 4 - 1))
    mixed = jax.random.permutation(jax.random.fold_in(own, 3), number_of)
    source_of, receiver = mixed[0:number_of // 2 * 2:2], mixed[1:number_of // 2 * 2:2]
    room = jnp.minimum(sizes[source_of] - 1, limit - sizes[receiver]) // 2
    room = jnp.where((source_of == sequence[0]) | (receiver == sequence[0]) | (sizes[receiver] == 0), 0, jnp.maximum(room, 0))
    moved = jax.random.randint(jax.random.fold_in(own, 4), (number_of // 2,), 0, 1 << 20) % (room + 1)
    sizes = sizes.at[source_of].add(-moved).at[receiver].add(moved)
    labels = jnp.searchsorted(jnp.cumsum(sizes), jnp.arange(rows * top), side="right").astype(jnp.int32)
    listing = labels.reshape(top, rows).T
    listing = listing[jax.random.permutation(jax.random.fold_in(own, 1), rows)]
    offset_by = jax.random.randint(jax.random.fold_in(own, 2), (rows, 1), 0, top)
    return jnp.take_along_axis(listing, (jnp.arange(top)[None, :] + offset_by) % top, axis=1)


def shares(count, total, bound, slope, full):
    loads = [(1 << 20) // math.isqrt(rank ** slope) + 1 for rank in range(1, count + 1)]
    largest = bound if full else min(bound, max(-(-total // count), total * loads[0] // sum(loads)))
    least = 1 if total - largest >= count - 1 else 0
    given, rest = [largest] + [least] * (count - 1), total - largest - least * (count - 1)
    while rest > 0:
        free = [i for i in range(1, count) if given[i] < largest] or [i for i in range(1, count) if given[i] < bound]
        mass, left = sum([loads[i] for i in free]), rest
        for i in free:
            extra = min(bound - given[i], max(1, left * loads[i] // mass), rest)
            given[i] = given[i] + extra
            rest = rest - extra
    return np.array(given)


def normal_values(rng, shape, scale, bound, cuts=(), kind=jnp.bfloat16):
    level = shard_levels(rng, shape, cuts, -0.22, 0.18) if cuts else 1.0
    result = jax.random.normal(rng, shape, jnp.float32) * scale * level
    return jnp.minimum(jnp.maximum(result, -bound), bound).astype(kind)


def setup_inputs(seed: int = 0) -> dict:
    splits = jax.random.split(jax.random.key(seed), 13)
    features = normal_values(splits[0], (B, D), 1.0, 6.0, ((0, 16), (1, 8)))
    cotangent = normal_values(splits[1], (B, D), 1.0, 6.0, ((0, 16), (1, 8)))
    cross_in = normal_values(splits[2], (D, RANK), D ** -0.5, 0.0625, ((0, 8),))
    cross_out = normal_values(splits[3], (D, RANK), RANK ** -0.5, 0.25, ((0, 8),))
    bias = normal_values(splits[4], (D,), 1.0, 6.0, ((0, 8),), jnp.float32)
    dest_shard_keys = jax.random.split(jax.random.fold_in(splits[5], 1), TABLES * B // B_DEV)
    dest_shard_turns = jax.random.permutation(jax.random.fold_in(splits[5], 3), TABLES * B // B_DEV)
    dest_shard = jax.vmap(lambda own, number: deal_out(jax.random.fold_in(splits[5], 2), own, number, B_DEV, N_ROW, 1, CAP, 2))(dest_shard_keys, dest_shard_turns).reshape((TABLES, B, 1))
    quot_row = place_ends(jax.random.randint(splits[6], (TABLES, B), 0, QR_DEV), jax.random.fold_in(splits[6], 1), 0, QR_DEV - 1).astype(jnp.int32)
    rem_row = place_ends(jax.random.randint(splits[7], (TABLES, B), 0, REM), jax.random.fold_in(splits[7], 1), 0, REM - 1).astype(jnp.int32)
    quot_slab = normal_values(splits[8], (TABLES, QROWS, EMB), 1.0, 6.0, ((0, 8), (1, 16)))
    quot_accum = jnp.clip(jnp.exp(math.log(2.0) - 3.6888794 * jax.random.uniform(splits[9], (TABLES, QROWS), jnp.float32) ** shard_levels(splits[9], (TABLES, QROWS), ((0, 8), (1, 16)), -0.2, 0.2)), 0.05, 2.0)
    rem_table = normal_values(splits[10], (TABLES, REM, EMB), 1.0, 6.0, ((0, 8),))
    rem_accum = jnp.clip(jnp.exp(math.log(20.0) - 3.6888795 * jax.random.uniform(splits[11], (TABLES, REM), jnp.float32) ** shard_levels(splits[11], (TABLES, REM), ((0, 8),), -0.2, 0.2)), 0.5, 20.0)
    return {"features": features, "cotangent": cotangent, "cross_in": cross_in, "cross_out": cross_out, "bias": bias, "dest_shard": dest_shard, "quot_row": quot_row, "rem_row": rem_row, "quot_slab": quot_slab, "quot_accum": quot_accum, "rem_table": rem_table, "rem_accum": rem_accum}


step_rate = 0.3
epsilon = 1e-06

def reference(features, cotangent, cross_in, cross_out, bias, dest_shard, quot_row, rem_row, quot_slab, quot_accum, rem_table, rem_accum):
    contract = (((1,), (1,)), ((), ()))

    def one_block(block):
        feats, cotan = block
        product = (cotan.astype(jnp.float32) * feats.astype(jnp.float32)).astype(jnp.bfloat16)
        rank_left = jnp.dot(feats, cross_in, preferred_element_type=jnp.float32).astype(jnp.bfloat16)
        rank_right = jnp.dot(product, cross_out, preferred_element_type=jnp.float32).astype(jnp.bfloat16)
        cross_gate = lax.dot_general(rank_left, cross_out, contract, preferred_element_type=jnp.float32) + bias
        cross_back = lax.dot_general(rank_right, cross_in, contract, preferred_element_type=jnp.float32)
        return (cotan.astype(jnp.float32) * (cross_gate + 1.0) + cross_back).astype(jnp.bfloat16)
    pooled = lax.map(one_block, (features.reshape(N_ROW, B_DEV, D), cotangent.reshape(N_ROW, B_DEV, D)))
    pooled = pooled.reshape(B, TABLES, EMB).transpose(1, 0, 2)

    def one_table(items):
        grads, target, qlocal, rlocal, slab, rtab = items
        qindex = target[:, 0] * QR_DEV + qlocal
        grad_q = jax.ops.segment_sum(grads.astype(jnp.float32) * rtab[rlocal].astype(jnp.float32), qindex, num_segments=QR_DEV * N_ROW)
        grad_r = jax.ops.segment_sum(grads.astype(jnp.float32) * slab[qindex].astype(jnp.float32), rlocal, num_segments=REM)
        return (grad_q, grad_r)
    quot_grad, rem_grad = lax.map(one_table, (pooled, dest_shard, quot_row, rem_row, quot_slab, rem_table))
    quot_acc_out = quot_accum + lax.optimization_barrier(jnp.mean(quot_grad * quot_grad, axis=-1))
    quot_out = (quot_slab.astype(jnp.float32) - step_rate * quot_grad * lax.rsqrt(quot_acc_out + epsilon)[..., None]).astype(jnp.bfloat16)
    rem_acc_out = rem_accum + lax.optimization_barrier(jnp.mean(rem_grad * rem_grad, axis=-1))
    rem_out = (rem_table.astype(jnp.float32) - step_rate * rem_grad * lax.rsqrt(rem_acc_out + epsilon)[..., None]).astype(jnp.bfloat16)
    return (quot_out, quot_acc_out, rem_out, rem_acc_out)
```

```python
import functools

import jax
import jax.numpy as jnp
from jax import lax
from jax.experimental import pallas as pl
from jax.experimental.pallas import tpu as pltpu
from jax.sharding import Mesh
from jax.sharding import PartitionSpec as P

step_rate = 0.3
epsilon = 1e-06
bf = jnp.bfloat16
f32 = jnp.float32
NX, NC, NZ, NY = 4, 2, 4, 4
CZY = ("c", "z", "y")
NT = (((1,), (1,)), ((), ()))


def ring(n, s):
    return [(i, (i + s) % n) for i in range(n)]


def spot(c, z, y):
    return (c * NZ + z) * NY + y


def turn_pairs(s, flip):
    out = []
    for c in range(NC):
        for z in range(NZ):
            for y in range(NY):
                if (c == 0) != flip:
                    to = spot(c, (z + s) % NZ, y)
                else:
                    to = spot(c, z, (y + s) % NY)
                out.append((spot(c, z, y), to))
    return out


def turn_groups(flip):
    out = []
    for c in range(NC):
        if (c == 0) != flip:
            out += [[spot(c, z, y) for z in range(NZ)] for y in range(NY)]
        else:
            out += [[spot(c, z, y) for y in range(NY)] for z in range(NZ)]
    return out


def pooled_kernel(rank_ref, cot_ref, co_ref, ci_ref, bias_ref, pos_ref, out_ref):
    rank = co_ref.shape[1]
    dests, tables, cap, width = out_ref.shape
    samples = cot_ref.shape[0]
    gate = (
        lax.dot_general(rank_ref[:, :rank], co_ref[...], NT, preferred_element_type=f32)
        + bias_ref[...]
    )
    back = lax.dot_general(rank_ref[:, rank:], ci_ref[...], NT, preferred_element_type=f32)
    pooled = (cot_ref[...].astype(f32) * (gate + 1.0) + back).astype(bf)
    slot = lax.broadcasted_iota(jnp.int32, (dests * cap, samples), 0)
    for t in range(tables):
        placed = jnp.where(slot == pos_ref[t], 1.0, 0.0).astype(bf)
        rows = jnp.dot(
            placed, pooled[:, t * width : (t + 1) * width], preferred_element_type=f32
        ).astype(bf)
        out_ref[:, t] = rows.reshape(dests, cap, width)


def pooled_dispatch(rank, cot, co, ci, bias, pos, dests, cap, width):
    samples = cot.shape[0]
    tables = pos.shape[0]
    pair = 2
    return pl.pallas_call(
        pooled_kernel,
        grid=(tables // pair,),
        out_shape=jax.ShapeDtypeStruct((dests, tables, cap, width), bf),
        in_specs=[
            pl.BlockSpec(rank.shape, lambda i: (0, 0)),
            pl.BlockSpec((samples, pair * width), lambda i: (0, i)),
            pl.BlockSpec((pair * width, co.shape[1]), lambda i: (i, 0)),
            pl.BlockSpec((pair * width, co.shape[1]), lambda i: (i, 0)),
            pl.BlockSpec((1, pair * width), lambda i: (0, i)),
            pl.BlockSpec((pair, 1, samples), lambda i: (i, 0, 0)),
        ],
        out_specs=pl.BlockSpec((dests, pair, cap, width), lambda i: (0, i, 0, 0)),
        name="pooled_dispatch",
    )(rank, cot, co, ci, bias, pos)


def table_kernel(core_ref, g_ref, krow_ref, kcol_ref, slab_ref, rtab_ref, rem_ref, quot_ref):
    sources, _, cap, width = g_ref.shape
    slots = sources * cap
    rem_rows = rtab_ref.shape[1]
    quot_rows = slab_ref.shape[1]
    rem_half = rem_rows // 2
    quot_half = quot_rows // 2
    g = g_ref[:, 0].reshape(slots, width).astype(f32)
    kcol = kcol_ref[0]
    krow = krow_ref[0]
    m_col, q_col = kcol % rem_rows, kcol // rem_rows
    m_row, q_row = krow % rem_rows, krow // rem_rows

    def pick(col, half, tab):
        hot = jnp.where(
            lax.broadcasted_iota(jnp.int32, (slots, half), 1) == col % half, 1.0, 0.0
        ).astype(bf)
        both = jnp.concatenate([tab[:half], tab[half:]], axis=1)
        got = jnp.dot(hot, both, preferred_element_type=f32)
        return jnp.where(col >= half, got[:, width:], got[:, :width])

    def spread(row, col, half, val):
        hot = jnp.where(
            lax.broadcasted_iota(jnp.int32, (half, slots), 0) == row % half, 1.0, 0.0
        ).astype(bf)
        both = jnp.concatenate(
            [jnp.where(col < half, val, 0.0), jnp.where(col >= half, val, 0.0)], axis=1
        ).astype(bf)
        return jnp.dot(hot, both, preferred_element_type=f32)

    quot_pick = pick(q_col, quot_half, slab_ref[0])
    rem_sum = spread(m_row, m_col, rem_half, g * quot_pick)
    first = core_ref[0] == 0
    sub_rows = rem_ref.shape[3]
    for z in range(NZ):
        for y in range(NY):
            start = (z * NY + y) * sub_rows
            at = start % rem_half
            side = start // rem_half
            block = rem_sum[at : at + sub_rows, side * width : (side + 1) * width]
            rem_ref[jnp.where(first, z, y), 0, jnp.where(first, y, z)] = block.astype(bf)
    rem_pick = pick(m_col, rem_half, rtab_ref[0])
    quot_sum = spread(q_row, q_col, quot_half, g * rem_pick)
    quot_ref[0, :quot_half] = quot_sum[:, :width]
    quot_ref[0, quot_half:] = quot_sum[:, width:]


def table_grads(core, g, keys, slab, rtab):
    sources, tables, cap, width = g.shape
    slots = sources * cap
    quot_rows, rem_rows = slab.shape[1], rtab.shape[1]
    sub = rem_rows // (NZ * NY)
    return pl.pallas_call(
        table_kernel,
        out_shape=(
            jax.ShapeDtypeStruct((NZ, tables, NY, sub, width), bf),
            jax.ShapeDtypeStruct((tables, quot_rows, width), f32),
        ),
        grid_spec=pltpu.PrefetchScalarGridSpec(
            num_scalar_prefetch=1,
            grid=(tables,),
            in_specs=[
                pl.BlockSpec((sources, 1, cap, width), lambda t, c: (0, t, 0, 0)),
                pl.BlockSpec((1, 1, slots), lambda t, c: (t, 0, 0)),
                pl.BlockSpec((1, slots, 1), lambda t, c: (t, 0, 0)),
                pl.BlockSpec((1, quot_rows, width), lambda t, c: (t, 0, 0)),
                pl.BlockSpec((1, rem_rows, width), lambda t, c: (t, 0, 0)),
            ],
            out_specs=(
                pl.BlockSpec((NZ, 1, NY, sub, width), lambda t, c: (0, t, 0, 0, 0)),
                pl.BlockSpec((1, quot_rows, width), lambda t, c: (t, 0, 0)),
            ),
        ),
        name="table_grads",
    )(core, g, keys.reshape(tables, 1, slots), keys.reshape(tables, slots, 1), slab, rtab)


def rank_sums(part):
    ci = lax.axis_index("c")
    xi = lax.axis_index("x")
    swap = [(0, 1), (1, 0)]
    half = part.shape[0] // NC
    size = half // NX
    keep = lax.dynamic_slice_in_dim(part, ci * half, half, 0)
    give = lax.dynamic_slice_in_dim(part, (1 - ci) * half, half, 0).astype(bf)
    got = lax.ppermute(give, "c", swap)
    both = (keep + got.astype(f32)).astype(bf).reshape(NX, size, -1)
    take = lambda k: lax.dynamic_index_in_dim(both, (xi + k) % NX, 0, keepdims=False)
    total = take(0).astype(f32)
    for k in (2, 1, 3):
        total = total + lax.ppermute(take(k), "x", ring(NX, k)).astype(f32)
    mine = total.astype(bf)
    parts = jnp.zeros_like(both)
    parts = lax.dynamic_update_index_in_dim(parts, mine, xi, 0)
    for k in (2, 1, 3):
        parts = lax.dynamic_update_index_in_dim(
            parts, lax.ppermute(mine, "x", ring(NX, k)), (xi - k) % NX, 0
        )
    own = parts.reshape(half, -1)
    other = lax.ppermute(own, "c", swap)
    low = jnp.where(ci == 0, own, other)
    high = jnp.where(ci == 0, other, own)
    return jnp.concatenate([low, high], axis=0)


def ring_gather(a, flip):
    ci = lax.axis_index("c")
    along_z = (ci == 0) != flip
    at = jnp.where(along_z, lax.axis_index("z"), lax.axis_index("y"))
    n = a.shape[0] // 2
    left = lax.ppermute(a, CZY, turn_pairs(1, flip))
    right = lax.ppermute(a, CZY, turn_pairs(-1, flip))
    far_low = lax.ppermute(left[:n], CZY, turn_pairs(1, flip))
    far_high = lax.ppermute(right[n:], CZY, turn_pairs(-1, flip))
    out = jnp.zeros((4,) + a.shape, a.dtype)
    out = lax.dynamic_update_index_in_dim(out, a, at, 0)
    out = lax.dynamic_update_index_in_dim(out, left, (at + 3) % 4, 0)
    out = lax.dynamic_update_index_in_dim(out, right, (at + 1) % 4, 0)
    zeros = (0,) * (a.ndim - 1)
    out = lax.dynamic_update_slice(out, far_low[None], ((at + 2) % 4, 0) + zeros)
    out = lax.dynamic_update_slice(out, far_high[None], ((at + 2) % 4, n) + zeros)
    return out


def per_device(
    features, cotangent, cross_in, cross_out, bias, dest_shard, quot_row, rem_row,
    quot_slab, quot_accum, rem_table, rem_accum,
):
    samples = features.shape[0]
    tables = quot_slab.shape[0]
    width = quot_slab.shape[2]
    rem_rows = rem_table.shape[1]
    rows = NZ * NY
    cap = 3 * samples // (2 * rows)
    slots = rows * cap
    ci, zi, yi = lax.axis_index("c"), lax.axis_index("z"), lax.axis_index("y")

    target = dest_shard[:, :, 0]
    onehot = target[:, :, None] == jnp.arange(rows, dtype=jnp.int32)[None, None, :]
    lower = (
        jnp.arange(samples, dtype=jnp.int32)[:, None]
        >= jnp.arange(samples, dtype=jnp.int32)[None, :]
    ).astype(bf)
    running = jnp.einsum("ij,tjn->tin", lower, onehot.astype(bf), preferred_element_type=f32)
    slot_index = jnp.sum(jnp.where(onehot, running, 0.0), axis=2).astype(jnp.int32) - 1
    position = target * cap + slot_index
    placed = position[:, :, None] == jnp.arange(slots, dtype=jnp.int32)[None, None, :]
    key_words = quot_row * rem_rows + rem_row
    send_keys = jnp.sum(jnp.where(placed, key_words[:, :, None], 0), axis=1)
    send_keys = send_keys.reshape(tables, rows, cap)
    got_keys = lax.all_to_all(send_keys, ("z", "y"), split_axis=1, concat_axis=1, tiled=True)
    got_keys = got_keys.reshape(tables, slots)

    product = (cotangent.astype(f32) * features.astype(f32)).astype(bf)
    part = jnp.concatenate(
        [
            jnp.dot(features, cross_in, preferred_element_type=f32),
            jnp.dot(product, cross_out, preferred_element_type=f32),
        ],
        axis=1,
    )
    rank = rank_sums(part)

    send = pooled_dispatch(
        rank, cotangent, cross_out, cross_in, bias.reshape(1, -1),
        position.reshape(tables, 1, samples), rows, cap, width,
    )
    got = lax.all_to_all(send, ("z", "y"), split_axis=0, concat_axis=0, tiled=True)
    rem_part, quot_grad = table_grads(ci.reshape(1), got, got_keys, quot_slab, rem_table)

    one = lax.all_to_all(
        rem_part, CZY, 0, 0, tiled=True, axis_index_groups=turn_groups(False)
    )
    one = jnp.sum(one.astype(f32), axis=0).astype(bf)
    two = lax.all_to_all(
        one.transpose(1, 0, 2, 3), CZY, 0, 0, tiled=True, axis_index_groups=turn_groups(True)
    )
    rem_grad = jnp.sum(two.astype(f32), axis=0)
    share = rem_rows // rows
    start = (zi * NY + yi) * share
    acc_in = lax.dynamic_slice_in_dim(rem_accum, start, share, 1)
    tab_in = lax.dynamic_slice_in_dim(rem_table, start, share, 1)
    rem_acc_out = acc_in + jnp.mean(rem_grad * rem_grad, axis=-1)
    rem_new = (
        tab_in.astype(f32) - step_rate * rem_grad * lax.rsqrt(rem_acc_out + epsilon)[..., None]
    ).astype(bf)
    four = ring_gather(rem_new, True)
    full = ring_gather(four.transpose(1, 0, 2, 3), False)
    rem_out = jnp.where(ci == 0, full.transpose(1, 0, 2, 3, 4), full.transpose(1, 2, 0, 3, 4))
    rem_out = rem_out.reshape(tables, rem_rows, width)

    quot_acc_out = quot_accum + jnp.mean(quot_grad * quot_grad, axis=-1)
    quot_out = (
        quot_slab.astype(f32)
        - step_rate * quot_grad * lax.rsqrt(quot_acc_out + epsilon)[..., None]
    ).astype(bf)
    return (quot_out, quot_acc_out, rem_out, rem_acc_out)


def solution(mesh):
    fine = Mesh(mesh.devices.reshape(NX, NC, NZ, NY), ("x", "c", "z", "y"))
    T, R = ("x", "c"), ("z", "y")
    return jax.shard_map(
        per_device,
        mesh=fine,
        in_specs=(
            P(R, T), P(R, T), P(T, None), P(T, None), P(T), P(T, R, None), P(T, R), P(T, R),
            P(T, R, None), P(T, R), P(T, None, None), P(T, None),
        ),
        out_specs=(P(T, R, None), P(T, R), P(T, None, None), P(T, R)),
        check_vma=False,
    )
```

```python
import functools

import jax
import jax.numpy as jnp
from jax import lax
from jax.experimental import pallas as pl
from jax.experimental.pallas import tpu as pltpu
from jax.sharding import Mesh
from jax.sharding import PartitionSpec as P

step_rate = 0.3
epsilon = 1e-06
bf = jnp.bfloat16
f32 = jnp.float32
NX, NC, NZ, NY = 4, 2, 4, 4
CZY = ("c", "z", "y")
NT = (((1,), (1,)), ((), ()))


def ring(n, s):
    return [(i, (i + s) % n) for i in range(n)]


def spot(c, z, y):
    return (c * NZ + z) * NY + y


def turn_pairs(s, flip):
    out = []
    for c in range(NC):
        for z in range(NZ):
            for y in range(NY):
                if (c == 0) != flip:
                    to = spot(c, (z + s) % NZ, y)
                else:
                    to = spot(c, z, (y + s) % NY)
                out.append((spot(c, z, y), to))
    return out


def turn_groups(flip):
    out = []
    for c in range(NC):
        if (c == 0) != flip:
            out += [[spot(c, z, y) for z in range(NZ)] for y in range(NY)]
        else:
            out += [[spot(c, z, y) for y in range(NY)] for z in range(NZ)]
    return out


def pooled_kernel(rank_ref, cot_ref, co_ref, ci_ref, bias_ref, pos_ref, dig_ref, out_ref, key_ref):
    rank = co_ref.shape[1]
    dests, tables, cap, width = out_ref.shape
    samples = cot_ref.shape[0]
    here = pos_ref.shape[0]
    step = pl.program_id(0)
    gate = (
        lax.dot_general(rank_ref[:, :rank], co_ref[...], NT, preferred_element_type=f32)
        + bias_ref[...]
    )
    back = lax.dot_general(rank_ref[:, rank:], ci_ref[...], NT, preferred_element_type=f32)
    pooled = (cot_ref[...].astype(f32) * (gate + 1.0) + back).astype(bf)
    slot = lax.broadcasted_iota(jnp.int32, (dests * cap, samples), 0)
    owner = lax.broadcasted_iota(jnp.int32, (samples, width), 1) // DIGITS
    keys = jnp.zeros((dests * cap, width), f32)
    for k in range(here):
        t = step * here + k
        placed = jnp.where(slot == pos_ref[k], 1.0, 0.0).astype(bf)
        digits = jnp.where(owner == t, dig_ref[...].astype(f32), 0.0).astype(bf)
        both = jnp.concatenate([pooled[:, k * width : (k + 1) * width], digits], axis=1)
        rows = jnp.dot(placed, both, preferred_element_type=f32)
        out_ref[:, t] = rows[:, :width].astype(bf).reshape(dests, cap, width)
        keys = keys + rows[:, width:]

    @pl.when(step == 0)
    def _():
        key_ref[...] = keys

    @pl.when(step > 0)
    def _():
        key_ref[...] += keys

    @pl.when(step == pl.num_programs(0) - 1)
    def _():
        out_ref[:, tables - 1] = key_ref[...].astype(bf).reshape(dests, cap, width)


def pooled_dispatch(rank, cot, co, ci, bias, pos, digits, dests, cap, width):
    samples = cot.shape[0]
    tables = pos.shape[0]
    pair = 2
    out = (dests, tables + 1, cap, width)
    return pl.pallas_call(
        pooled_kernel,
        grid=(tables // pair,),
        out_shape=jax.ShapeDtypeStruct(out, bf),
        in_specs=[
            pl.BlockSpec(rank.shape, lambda i: (0, 0)),
            pl.BlockSpec((samples, pair * width), lambda i: (0, i)),
            pl.BlockSpec((pair * width, co.shape[1]), lambda i: (i, 0)),
            pl.BlockSpec((pair * width, co.shape[1]), lambda i: (i, 0)),
            pl.BlockSpec((1, pair * width), lambda i: (0, i)),
            pl.BlockSpec((pair, 1, samples), lambda i: (i, 0, 0)),
            pl.BlockSpec(digits.shape, lambda i: (0, 0)),
        ],
        out_specs=pl.BlockSpec(out, lambda i: (0, 0, 0, 0)),
        scratch_shapes=[pltpu.VMEM((dests * cap, width), f32)],
        name="pooled_dispatch",
    )(rank, cot, co, ci, bias, pos, digits)


DIGITS, QB, MB = 4, 32, 64


def digit_lanes(q, m, width):
    parts = jnp.stack([q // QB, q % QB, m // MB, m % MB], axis=1)
    parts = parts.reshape(-1, q.shape[1])
    parts = jnp.pad(parts, ((0, width - parts.shape[0]), (0, 0)))
    return parts.T.astype(bf)


def key_rows(keys, tables):
    width = keys.shape[1]
    lane = lax.broadcasted_iota(jnp.int32, (width, width), 0)
    col = lax.broadcasted_iota(jnp.int32, (width, width), 1)
    t = col % tables
    base = DIGITS * t + jnp.where(col >= tables, 2, 0)
    high = jnp.where(col >= tables, MB, QB).astype(f32)
    comb = jnp.where(lane == base, high, jnp.where(lane == base + 1, 1.0, 0.0))
    comb = jnp.where(col < 2 * tables, comb, 0.0).astype(bf)
    return jnp.dot(keys, comb, preferred_element_type=f32).T


def key_lanes(keys, t):
    width = keys.shape[1]
    lane = lax.broadcasted_iota(jnp.int32, (width, 2 * width), 0) - DIGITS * t
    side = lax.broadcasted_iota(jnp.int32, (width, 2 * width), 1) >= width
    lane = jnp.where(side, lane - 2, lane)
    high = jnp.where(side, float(MB), float(QB))
    comb = jnp.where(lane == 0, high, jnp.where(lane == 1, 1.0, 0.0)).astype(bf)
    out = jnp.dot(keys, comb, preferred_element_type=f32)
    return out[:, :width], out[:, width:]


def pick(key, tab):
    slots, width = key.shape
    half = tab.shape[0] // 2
    high = key >= half
    low = jnp.where(high, key - half, key)
    lane = lax.broadcasted_iota(jnp.int32, (slots, width), 1).astype(f32)
    hot = jnp.concatenate(
        [jnp.where(low - j == lane, 1.0, 0.0).astype(bf) for j in range(0, half, width)], axis=1
    )
    both = jnp.concatenate([tab[:half], tab[half:]], axis=1)
    got = jnp.dot(hot, both, preferred_element_type=f32)
    return jnp.where(high, got[:, width:], got[:, :width])


def spread(row, key, rows, val):
    slots = row.shape[1]
    half = rows // 2
    low = jnp.where(row >= half, row - half, row)
    at = lax.broadcasted_iota(jnp.int32, (half, slots), 0).astype(f32)
    hot = jnp.where(at == low, 1.0, 0.0).astype(bf)
    high = key >= half
    both = jnp.concatenate(
        [jnp.where(high, 0.0, val).astype(bf), jnp.where(high, val, 0.0).astype(bf)], axis=1
    )
    return jnp.dot(hot, both, preferred_element_type=f32)


def rem_kernel(first, tables, where_ref, g_ref, key_ref, slab_ref, r0, r1, r2, r3, row_ref, sum_ref):
    sources, _, cap, width = g_ref.shape
    slots = sources * cap
    rem_rows = sum_ref.shape[0]
    step = pl.program_id(0)
    keys = key_ref[:, 0].reshape(slots, width)

    @pl.when(step == 0)
    def _():
        row_ref[...] = key_rows(keys, tables)

    t = first + step
    g = g_ref[:, 0].reshape(slots, width).astype(f32)
    q, m = key_lanes(keys, t)
    val = g * pick(q, slab_ref[0])
    both = spread(row_ref[pl.ds(tables + t, 1), :], m, rem_rows, val)
    sum_ref[: rem_rows // 2] = both[:, :width].astype(bf)
    sum_ref[rem_rows // 2 :] = both[:, width:].astype(bf)
    sub_rows = r0.shape[2]
    at = where_ref[1]
    along_z = where_ref[0] == 0
    for rel, ref in enumerate((r0, r1, r2, r3)):
        far = (at + rel) % 4
        for sub in range(4):
            block = jnp.where(along_z, far * NY + sub, sub * NY + far)
            start = pl.multiple_of(block * sub_rows, sub_rows)
            ref[0, sub] = sum_ref[pl.ds(start, sub_rows), :]


def rem_parts(first, count, where, got, slab, rem_rows):
    sources, tables, cap, width = got.shape
    tables -= 1
    slots = sources * cap
    quot_rows = slab.shape[1]
    sub = rem_rows // (NZ * NY)
    piece = jax.ShapeDtypeStruct((count, 4, sub, width), bf)
    return pl.pallas_call(
        functools.partial(rem_kernel, first, tables),
        out_shape=(piece,) * 4,
        grid_spec=pltpu.PrefetchScalarGridSpec(
            num_scalar_prefetch=1,
            grid=(count,),
            in_specs=[
                pl.BlockSpec((sources, 1, cap, width), lambda t, c: (0, first + t, 0, 0)),
                pl.BlockSpec((sources, 1, cap, width), lambda t, c: (0, tables, 0, 0)),
                pl.BlockSpec((1, quot_rows, width), lambda t, c: (first + t, 0, 0)),
            ],
            out_specs=[pl.BlockSpec((1, 4, sub, width), lambda t, c: (t, 0, 0, 0))] * 4,
            scratch_shapes=[pltpu.VMEM((width, slots), f32), pltpu.VMEM((rem_rows, width), bf)],
        ),
        cost_estimate=pl.CostEstimate(
            flops=count * 4 * slots * rem_rows * width, bytes_accessed=1 << 22, transcendentals=0
        ),
        name="rem_parts",
    )(where, got, got, slab)


def quot_kernel(tables, g_ref, key_ref, rtab_ref, quot_ref, row_ref):
    sources, _, cap, width = g_ref.shape
    slots = sources * cap
    quot_rows = quot_ref.shape[1]
    t = pl.program_id(0)
    keys = key_ref[:, 0].reshape(slots, width)

    @pl.when(t == 0)
    def _():
        row_ref[...] = key_rows(keys, tables)

    g = g_ref[:, 0].reshape(slots, width).astype(f32)
    q, m = key_lanes(keys, t)
    val = g * pick(m, rtab_ref[0])
    both = spread(row_ref[pl.ds(t, 1), :], q, quot_rows, val)
    quot_ref[0, : quot_rows // 2] = both[:, :width]
    quot_ref[0, quot_rows // 2 :] = both[:, width:]


def quot_grads(got, rtab, quot_rows):
    sources, tables, cap, width = got.shape
    tables -= 1
    slots = sources * cap
    rem_rows = rtab.shape[1]
    return pl.pallas_call(
        functools.partial(quot_kernel, tables),
        out_shape=jax.ShapeDtypeStruct((tables, quot_rows, width), f32),
        grid=(tables,),
        in_specs=[
            pl.BlockSpec((sources, 1, cap, width), lambda t: (0, t, 0, 0)),
            pl.BlockSpec((sources, 1, cap, width), lambda t: (0, tables, 0, 0)),
            pl.BlockSpec((1, rem_rows, width), lambda t: (t, 0, 0)),
        ],
        out_specs=pl.BlockSpec((1, quot_rows, width), lambda t: (t, 0, 0)),
        scratch_shapes=[pltpu.VMEM((width, slots), f32)],
        cost_estimate=pl.CostEstimate(
            flops=tables * 4 * slots * rem_rows * width, bytes_accessed=1 << 23, transcendentals=0
        ),
        name="quot_grads",
    )(got, got, rtab)


def turn(a, s, flip):
    return lax.ppermute(a, CZY, turn_pairs(s, flip))


def add(*parts):
    total = parts[0].astype(f32)
    for p in parts[1:]:
        total = total + p.astype(f32)
    return total


def ring_scatter(low, high, flip):
    far_low = turn(low[2], 1, flip)
    far_high = turn(high[2], -1, flip)
    near_low = turn(low[3], -1, flip)
    near_high = turn(high[1], 1, flip)
    sum_low = turn(add(low[1], far_low).astype(bf), 1, flip)
    sum_high = turn(add(high[3], far_high).astype(bf), -1, flip)
    return add(low[0], near_low, sum_low), add(high[0], near_high, sum_high)


def ring_gather(low, high, flip):
    prev_low = turn(low, 1, flip)
    next_high = turn(high, -1, flip)
    prev_high = turn(high, 1, flip)
    next_low = turn(low, -1, flip)
    far_low = turn(prev_low, 1, flip)
    far_high = turn(next_high, -1, flip)
    return [low, next_low, far_low, prev_low], [high, next_high, far_high, prev_high]


def place_kernel(rels, where_ref, *refs):
    out_ref = refs[-1]
    half = out_ref.shape[0] // 2
    for k in range(len(rels)):

        @pl.when(pl.program_id(0) == k)
        def _():
            out_ref[:half, 0, 0] = refs[2 * k][:, 0]
            out_ref[half:, 0, 0] = refs[2 * k + 1][:, 0]


def place(rels, where, pieces, shape, old=None):
    tables, _, _, sub, width = shape
    half = tables // 2

    def out_map(k, s, w):
        rel = sum(jnp.where(k == i, r, 0) for i, r in enumerate(rels))
        far = (w[2] + rel) % 4
        along_z = w[0] == 0
        return 0, jnp.where(along_z, far, s), jnp.where(along_z, s, far), 0, 0

    ins = [x for lh in pieces for x in lh]
    specs = [
        pl.BlockSpec(
            (half, 1, sub, width),
            lambda k, s, w, i=i: (0, jnp.where(k < i, 0, jnp.where(k > i, 3, s)), 0, 0),
        )
        for i in range(len(rels))
        for _ in range(2)
    ]
    alias = {}
    if old is not None:
        ins.append(old)
        specs.append(pl.BlockSpec(memory_space=pl.ANY))
        alias = {len(ins): 0}
    return pl.pallas_call(
        functools.partial(place_kernel, rels),
        out_shape=jax.ShapeDtypeStruct(shape, bf),
        grid_spec=pltpu.PrefetchScalarGridSpec(
            num_scalar_prefetch=1,
            grid=(len(rels), 4),
            in_specs=specs,
            out_specs=pl.BlockSpec((tables, 1, 1, sub, width), out_map),
        ),
        input_output_aliases=alias,
        cost_estimate=pl.CostEstimate(flops=0, bytes_accessed=len(rels) << 21, transcendentals=0),
        name="place",
    )(where, *ins)


def rank_sums(part):
    ci = lax.axis_index("c")
    xi = lax.axis_index("x")
    swap = [(0, 1), (1, 0)]
    half = part.shape[0] // NC
    size = half // NX
    keep = lax.dynamic_slice_in_dim(part, ci * half, half, 0)
    give = lax.dynamic_slice_in_dim(part, (1 - ci) * half, half, 0).astype(bf)
    got = lax.ppermute(give, "c", swap)
    both = (keep + got.astype(f32)).astype(bf).reshape(NX, size, -1)
    take = lambda k: lax.dynamic_index_in_dim(both, (xi + k) % NX, 0, keepdims=False)
    total = take(0).astype(f32)
    for k in (2, 1, 3):
        total = total + lax.ppermute(take(k), "x", ring(NX, k)).astype(f32)
    mine = total.astype(bf)
    parts = jnp.zeros_like(both)
    parts = lax.dynamic_update_index_in_dim(parts, mine, xi, 0)
    for k in (2, 1, 3):
        parts = lax.dynamic_update_index_in_dim(
            parts, lax.ppermute(mine, "x", ring(NX, k)), (xi - k) % NX, 0
        )
    own = parts.reshape(half, -1)
    other = lax.ppermute(own, "c", swap)
    low = jnp.where(ci == 0, own, other)
    high = jnp.where(ci == 0, other, own)
    return jnp.concatenate([low, high], axis=0)


def per_device(
    features, cotangent, cross_in, cross_out, bias, dest_shard, quot_row, rem_row,
    quot_slab, quot_accum, rem_table, rem_accum,
):
    samples = features.shape[0]
    tables = quot_slab.shape[0]
    width = quot_slab.shape[2]
    rem_rows = rem_table.shape[1]
    rows = NZ * NY
    cap = 3 * samples // (2 * rows)
    slots = rows * cap
    ci, zi, yi = lax.axis_index("c"), lax.axis_index("z"), lax.axis_index("y")

    target = dest_shard[:, :, 0]
    onehot = target[:, :, None] == jnp.arange(rows, dtype=jnp.int32)[None, None, :]
    lower = (
        jnp.arange(samples, dtype=jnp.int32)[:, None]
        >= jnp.arange(samples, dtype=jnp.int32)[None, :]
    ).astype(bf)
    running = jnp.einsum("ij,tjn->tin", lower, onehot.astype(bf), preferred_element_type=f32)
    slot_index = jnp.sum(jnp.where(onehot, running, 0.0), axis=2).astype(jnp.int32) - 1
    position = target * cap + slot_index
    digits = digit_lanes(quot_row, rem_row, width)

    product = (cotangent.astype(f32) * features.astype(f32)).astype(bf)
    part = jnp.concatenate(
        [
            jnp.dot(features, cross_in, preferred_element_type=f32),
            jnp.dot(product, cross_out, preferred_element_type=f32),
        ],
        axis=1,
    )
    rank = rank_sums(part)

    send = pooled_dispatch(
        rank, cotangent, cross_out, cross_in, bias.reshape(1, -1),
        position.reshape(tables, 1, samples), digits, rows, cap, width,
    )
    got = lax.all_to_all(send, ("z", "y"), split_axis=0, concat_axis=0, tiled=True)
    along_z = ci == 0
    at_one = jnp.where(along_z, zi, yi)
    at_two = jnp.where(along_z, yi, zi)
    where = jnp.stack([ci, at_one, at_one]).astype(jnp.int32)
    half = tables // 2
    low = rem_parts(0, half, where, got, quot_slab, rem_rows)
    high = rem_parts(half, half, where, got, quot_slab, rem_rows)

    one_low, one_high = ring_scatter(low, high, False)
    ring_low, ring_high = ring_gather(one_low.astype(bf), one_high.astype(bf), True)
    share = rem_rows // rows
    view = (tables, NZ, NY, share)

    def quarter(a):
        a = a.reshape(view + a.shape[2:])
        return jnp.where(
            along_z,
            lax.dynamic_index_in_dim(a, zi, 1, keepdims=False),
            lax.dynamic_index_in_dim(a, yi, 2, keepdims=False),
        )

    def update(ring, acc_in, tab_in):
        grad = (ring[0].astype(f32) + ring[2].astype(f32)) + (
            ring[1].astype(f32) + ring[3].astype(f32)
        )
        acc = acc_in + jnp.mean(grad * grad, axis=-1)
        new = tab_in.astype(f32) - step_rate * grad * lax.rsqrt(acc + epsilon)[..., None]
        return acc, new.astype(bf)

    acc_in, tab_in = quarter(rem_accum), quarter(rem_table)
    acc_low, new_low = update(ring_low, acc_in[:half], tab_in[:half])
    acc_high, new_high = update(ring_high, acc_in[half:], tab_in[half:])
    acc = jnp.concatenate([acc_low, acc_high], axis=0)
    rem_acc_out = lax.dynamic_index_in_dim(acc, at_two, 1, keepdims=False)
    all_low, all_high = ring_gather(new_low, new_high, False)
    shape = (tables, NZ, NY, share, width)
    near = [(all_low[k], all_high[k]) for k in (0, 1, 3)]
    rem_out = place((0, 1, 3), where, near, shape)
    rem_out = place((2,), where, [(all_low[2], all_high[2])], shape, rem_out)
    rem_out = rem_out.reshape(tables, rem_rows, width)

    quot_grad = quot_grads(got, rem_table, quot_slab.shape[1])
    quot_acc_out = quot_accum + jnp.mean(quot_grad * quot_grad, axis=-1)
    quot_out = (
        quot_slab.astype(f32)
        - step_rate * quot_grad * lax.rsqrt(quot_acc_out + epsilon)[..., None]
    ).astype(bf)
    return (quot_out, quot_acc_out, rem_out, rem_acc_out)


def solution(mesh):
    fine = Mesh(mesh.devices.reshape(NX, NC, NZ, NY), ("x", "c", "z", "y"))
    T, R = ("x", "c"), ("z", "y")
    return jax.shard_map(
        per_device,
        mesh=fine,
        in_specs=(
            P(R, T), P(R, T), P(T, None), P(T, None), P(T), P(T, R, None), P(T, R), P(T, R),
            P(T, R, None), P(T, R), P(T, None, None), P(T, None),
        ),
        out_specs=(P(T, R, None), P(T, R), P(T, None, None), P(T, R)),
        check_vma=False,
    )
```

```python
import functools

import jax
import jax.numpy as jnp
from jax import lax
from jax.experimental import pallas as pl
from jax.experimental.pallas import tpu as pltpu
from jax.sharding import Mesh
from jax.sharding import PartitionSpec as P


step_rate = 0.3
epsilon = 1e-06
bf = jnp.bfloat16
f32 = jnp.float32
NX, NC, NZ, NY = 4, 2, 4, 4
CZY = ("c", "z", "y")
NT = (((1,), (1,)), ((), ()))


def ring(n, s):
    return [(i, (i + s) % n) for i in range(n)]


def spot(c, z, y):
    return (c * NZ + z) * NY + y


def turn_pairs(s, flip):
    out = []
    for c in range(NC):
        for z in range(NZ):
            for y in range(NY):
                if (c == 0) != flip:
                    to = spot(c, (z + s) % NZ, y)
                else:
                    to = spot(c, z, (y + s) % NY)
                out.append((spot(c, z, y), to))
    return out


def rank_kernel(half_ref, feat_ref, cot_ref, ci_ref, co_ref, out_ref, acc_ref):
    step = pl.program_id(0)
    rank = ci_ref.shape[1]
    feat = feat_ref[...]
    product = (cot_ref[...].astype(f32) * feat.astype(f32)).astype(bf)

    @pl.when(step == 0)
    def _():
        acc_ref[...] = jnp.zeros_like(acc_ref)

    acc_ref[:, :rank] += jnp.dot(feat, ci_ref[...], preferred_element_type=f32)
    acc_ref[:, rank:] += jnp.dot(product, co_ref[...], preferred_element_type=f32)

    @pl.when(step == pl.num_programs(0) - 1)
    def _():
        out_ref[...] = acc_ref[...].astype(out_ref.dtype)


def rank_part(half, feat, cot, ci, co, dtype):
    size = feat.shape[0] // NC
    depth, rank = ci.shape
    tile = depth // 4
    return pl.pallas_call(
        rank_kernel,
        out_shape=jax.ShapeDtypeStruct((size, 2 * rank), dtype),
        grid_spec=pltpu.PrefetchScalarGridSpec(
            num_scalar_prefetch=1,
            grid=(depth // tile,),
            in_specs=[
                pl.BlockSpec((size, tile), lambda k, h: (h[0], k)),
                pl.BlockSpec((size, tile), lambda k, h: (h[0], k)),
                pl.BlockSpec((tile, rank), lambda k, h: (k, 0)),
                pl.BlockSpec((tile, rank), lambda k, h: (k, 0)),
            ],
            out_specs=pl.BlockSpec((size, 2 * rank), lambda k, h: (0, 0)),
            scratch_shapes=[pltpu.VMEM((size, 2 * rank), f32)],
        ),
        cost_estimate=pl.CostEstimate(
            flops=4 * size * depth * rank, bytes_accessed=4 << 20, transcendentals=0
        ),
        compiler_params=pltpu.CompilerParams(vmem_limit_bytes=16 << 20),
        name="rank_part",
    )(half, feat, cot, ci, co)


def mix_kernel(x_ref, keep_ref, got_ref, *outs):
    size = outs[0].shape[0]
    for k, out in enumerate(outs):
        at = pl.ds(pl.multiple_of((x_ref[0] + k) % NX * size, size), size)
        out[...] = (keep_ref[at, :] + got_ref[at, :].astype(f32)).astype(bf)


def mix(xi, keep, got):
    piece = jax.ShapeDtypeStruct((keep.shape[0] // NX, keep.shape[1]), bf)
    vmem = pl.BlockSpec(memory_space=pltpu.VMEM)
    return pl.pallas_call(
        mix_kernel,
        out_shape=(piece,) * NX,
        grid_spec=pltpu.PrefetchScalarGridSpec(
            num_scalar_prefetch=1, grid=(), in_specs=[vmem] * 2, out_specs=[vmem] * NX
        ),
        compiler_params=pltpu.CompilerParams(vmem_limit_bytes=8 << 20),
        name="mix",
    )(xi, keep, got)


def pooled_kernel(at_ref, *refs):
    pieces, (cot_ref, co_ref, ci_ref, bias_ref, pos_ref, dig_ref, out_ref, key_ref, rank_ref) = (
        refs[: NC * NX],
        refs[NC * NX :],
    )
    rank = co_ref.shape[1]
    width, cap = key_ref.shape[1], CAP

    @pl.when(pl.program_id(0) == 0)
    def _():
        size = pieces[0].shape[0]
        for i, piece in enumerate(pieces):
            c = at_ref[0] if i < NX else 1 - at_ref[0]
            row = (c * NX + (at_ref[1] + NX - i % NX) % NX) * size
            rank_ref[pl.ds(pl.multiple_of(row, size), size), :] = piece[...]

    dests = out_ref.shape[0]
    tables = (out_ref.shape[1] - KEY_ROWS) // cap
    samples = cot_ref.shape[0]
    here = pos_ref.shape[0]
    step = pl.program_id(0)
    gate = (
        lax.dot_general(rank_ref[:, :rank], co_ref[...], NT, preferred_element_type=f32)
        + bias_ref[...]
    )
    back = lax.dot_general(rank_ref[:, rank:], ci_ref[...], NT, preferred_element_type=f32)
    pooled = (cot_ref[...].astype(f32) * (gate + 1.0) + back).astype(bf)
    slot = lax.broadcasted_iota(jnp.int32, (dests * cap, samples), 0)
    owner = lax.broadcasted_iota(jnp.int32, (samples, width), 1) % LANES // DIGITS
    keys = jnp.zeros((dests * cap, width), f32)
    for k in range(here):
        t = step * here + k
        placed = jnp.where(slot == pos_ref[k], 1.0, 0.0).astype(bf)
        digits = jnp.where(owner == t, dig_ref[...].astype(f32), 0.0).astype(bf)
        both = jnp.concatenate([pooled[:, k * width : (k + 1) * width], digits], axis=1)
        rows = jnp.dot(placed, both, preferred_element_type=f32)
        spot = pl.ds(pl.multiple_of(t * cap, KEY_ROWS), cap)
        out_ref[:, spot] = rows[:, :width].astype(bf).reshape(dests, cap, width)
        keys = keys + rows[:, width:]

    @pl.when(step == 0)
    def _():
        key_ref[...] = keys

    @pl.when(step > 0)
    def _():
        key_ref[...] += keys

    @pl.when(step == pl.num_programs(0) - 1)
    def _():
        parts = key_ref[...].reshape(dests, cap // KEY_ROWS, KEY_ROWS, width)
        group = lax.broadcasted_iota(jnp.int32, (dests, KEY_ROWS, width), 2) // LANES
        packed = jnp.zeros((dests, KEY_ROWS, width), f32)
        for k in range(cap // KEY_ROWS):
            packed = jnp.where(group == k, parts[:, k], packed)
        out_ref[:, tables * cap :] = packed.astype(bf)


def pooled_dispatch(where, pieces, cot, co, ci, bias, pos, digits, dests, cap, width):
    samples = cot.shape[0]
    tables = pos.shape[0]
    pair = 2
    out = (dests, tables * cap + KEY_ROWS, width)
    return pl.pallas_call(
        pooled_kernel,
        out_shape=jax.ShapeDtypeStruct(out, bf),
        grid_spec=pltpu.PrefetchScalarGridSpec(
            num_scalar_prefetch=1,
            grid=(tables // pair,),
            in_specs=[pl.BlockSpec(memory_space=pltpu.VMEM)] * len(pieces)
            + [
                pl.BlockSpec((samples, pair * width), lambda i, w: (0, i)),
                pl.BlockSpec((pair * width, co.shape[1]), lambda i, w: (i, 0)),
                pl.BlockSpec((pair * width, co.shape[1]), lambda i, w: (i, 0)),
                pl.BlockSpec((1, pair * width), lambda i, w: (0, i)),
                pl.BlockSpec((pair, 1, samples), lambda i, w: (i, 0, 0)),
                pl.BlockSpec(digits.shape, lambda i, w: (0, 0)),
            ],
            out_specs=pl.BlockSpec(out, lambda i, w: (0, 0, 0)),
            scratch_shapes=[
                pltpu.VMEM((dests * cap, width), f32),
                pltpu.VMEM((samples, pieces[0].shape[1]), bf),
            ],
        ),
        compiler_params=pltpu.CompilerParams(vmem_limit_bytes=16 << 20),
        name="pooled_dispatch",
    )(where, *pieces, cot, co, ci, bias, pos, digits)


DIGITS, QB, MB, LANES, KEY_ROWS, CAP = 4, 32, 64, 32, 16, 48
PARTS = 2


def digit_lanes(q, m, width):
    parts = jnp.stack([q // QB, q % QB, m // MB, m % MB], axis=1)
    parts = parts.reshape(-1, q.shape[1])
    parts = jnp.concatenate([parts] * (CAP // KEY_ROWS), axis=0)
    parts = jnp.pad(parts, ((0, width - parts.shape[0]), (0, 0)))
    return parts.T.astype(bf)


def unpack_keys(packed):
    sources, _, width = packed.shape
    group = lax.broadcasted_iota(jnp.int32, packed.shape, 2) // LANES
    packed = packed.astype(f32)
    parts = [jnp.where(group == k, packed, 0.0)[:, None] for k in range(CAP // KEY_ROWS)]
    return jnp.concatenate(parts, axis=1).reshape(sources * CAP, width).astype(bf)


def key_rows(keys, tables):
    width = keys.shape[1]
    lane = lax.broadcasted_iota(jnp.int32, (width, width), 0) % LANES
    col = lax.broadcasted_iota(jnp.int32, (width, width), 1)
    t = col % tables
    base = DIGITS * t + jnp.where(col >= tables, 2, 0)
    high = jnp.where(col >= tables, MB, QB).astype(f32)
    comb = jnp.where(lane == base, high, jnp.where(lane == base + 1, 1.0, 0.0))
    comb = jnp.where(col < 2 * tables, comb, 0.0).astype(bf)
    return jnp.dot(keys, comb, preferred_element_type=f32).T


def key_lanes(keys, t):
    width = keys.shape[1]
    lane = lax.broadcasted_iota(jnp.int32, (width, 2 * width), 0) % LANES - DIGITS * t
    side = lax.broadcasted_iota(jnp.int32, (width, 2 * width), 1) >= width
    lane = jnp.where(side, lane - 2, lane)
    high = jnp.where(side, float(MB), float(QB))
    comb = jnp.where(lane == 0, high, jnp.where(lane == 1, 1.0, 0.0)).astype(bf)
    out = jnp.dot(keys, comb, preferred_element_type=f32)
    return out[:, :width], out[:, width:]


def pick(key, tab):
    slots, width = key.shape
    half = tab.shape[0] // 2
    both = jnp.concatenate([tab[:half], tab[half:]], axis=1)
    size = slots // PARTS
    out = []
    for p in range(PARTS):
        part = key[p * size : (p + 1) * size]
        high = part >= half
        low = jnp.where(high, part - half, part)
        lane = lax.broadcasted_iota(jnp.int32, (size, width), 1).astype(f32)
        hot = jnp.concatenate(
            [jnp.where(low - j == lane, 1.0, 0.0).astype(bf) for j in range(0, half, width)],
            axis=1,
        )
        got = jnp.dot(hot, both, preferred_element_type=f32)
        out.append(jnp.where(high, got[:, width:], got[:, :width]))
    return jnp.concatenate(out, axis=0)


def spread(row, key, rows, val, store):
    slots = row.shape[1]
    width = val.shape[1]
    half = rows // 2
    low = jnp.where(row >= half, row - half, row)
    high = key >= half
    both = jnp.concatenate(
        [jnp.where(high, 0.0, val).astype(bf), jnp.where(high, val, 0.0).astype(bf)], axis=1
    )
    size = half // PARTS
    at = lax.broadcasted_iota(jnp.int32, (size, slots), 0).astype(f32)
    for p in range(PARTS):
        hot = jnp.where(at == low - p * size, 1.0, 0.0).astype(bf)
        sums = jnp.dot(hot, both, preferred_element_type=f32)
        store(p * size, sums[:, :width])
        store(half + p * size, sums[:, width:])


def rem_kernel(
    first, tables, where_ref, got_ref, slab_ref, r0, r1, r2, r3,
    g_buf, pack_buf, slab_buf, sum_ref, sem, pack_sem,
):
    count, sources, cap, width = g_buf.shape
    slots = sources * cap
    rem_rows = sum_ref.shape[0]
    pack = pltpu.make_async_copy(
        got_ref.at[:, pl.ds(tables * cap, KEY_ROWS)], pack_buf, pack_sem
    )
    pack.start()

    def inputs(k):
        return (
            pltpu.make_async_copy(
                got_ref.at[:, pl.ds((first + k) * cap, cap)], g_buf.at[k], sem.at[0, k]
            ),
            pltpu.make_async_copy(slab_ref.at[first + k], slab_buf.at[k], sem.at[1, k]),
        )

    copies = [inputs(k) for k in range(count)]
    for pair in copies:
        for copy in pair:
            copy.start()
    pack.wait()
    keys = unpack_keys(pack_buf[...])
    rows = key_rows(keys, tables)
    sub_rows = r0.shape[2]
    at = where_ref[1]
    along_z = where_ref[0] == 0
    for k in range(count):
        for copy in copies[k]:
            copy.wait()
        t = first + k
        g = g_buf[k].reshape(slots, width).astype(f32)
        q, m = key_lanes(keys, t)
        val = g * pick(q, slab_buf[k])


        def store(at, sums):
            sum_ref[at : at + sums.shape[0]] = sums.astype(bf)

        spread(rows[tables + t : tables + t + 1], m, rem_rows, val, store)
        for rel, ref in enumerate((r0, r1, r2, r3)):
            far = (at + rel) % 4
            for sub in range(4):
                block = jnp.where(along_z, far * NY + sub, sub * NY + far)
                start = pl.multiple_of(block * sub_rows, sub_rows)
                ref[k, sub] = sum_ref[pl.ds(start, sub_rows), :]


def rem_parts(first, count, where, got, slab, rem_rows):
    sources, _, width = got.shape
    tables, quot_rows, _ = slab.shape
    slots = sources * CAP
    slab = pltpu.with_memory_space_constraint(slab, pltpu.HBM)
    sub = rem_rows // (NZ * NY)
    piece = jax.ShapeDtypeStruct((count, 4, sub, width), bf)
    return pl.pallas_call(
        functools.partial(rem_kernel, first, tables),
        out_shape=(piece,) * 4,
        grid_spec=pltpu.PrefetchScalarGridSpec(
            num_scalar_prefetch=1,
            grid=(),
            in_specs=[
                pl.BlockSpec(memory_space=pl.ANY),
                pl.BlockSpec(memory_space=pltpu.HBM),
            ],
            out_specs=[pl.BlockSpec(memory_space=pltpu.VMEM)] * 4,
            scratch_shapes=[
                pltpu.VMEM((count, sources, CAP, width), bf),
                pltpu.VMEM((sources, KEY_ROWS, width), bf),
                pltpu.VMEM((count, quot_rows, width), bf),
                pltpu.VMEM((rem_rows, width), bf),
                pltpu.SemaphoreType.DMA((2, count)),
                pltpu.SemaphoreType.DMA,
            ],
        ),
        cost_estimate=pl.CostEstimate(
            flops=count * 4 * slots * rem_rows * width, bytes_accessed=1 << 22, transcendentals=0
        ),
        compiler_params=pltpu.CompilerParams(vmem_limit_bytes=16 << 20),
        name="rem_parts",
    )(where, got, slab)


def quot_kernel(first, tables, g_ref, pack_ref, rtab_ref, *refs):
    quot_ref, key_ref, row_ref = refs[-3:]
    sources, cap, width = g_ref.shape
    slots = sources * cap
    quot_rows = quot_ref.shape[1]
    step = pl.program_id(0)
    t = first + step

    @pl.when(step == 0)
    def _():
        keys = unpack_keys(pack_ref[...])
        key_ref[...] = keys
        row_ref[...] = key_rows(keys, tables)

    g = g_ref[...].reshape(slots, width).astype(f32)
    q, m = key_lanes(key_ref[...], t)
    val = g * pick(m, rtab_ref[0])

    def store(at, sums):
        quot_ref[0, at : at + sums.shape[0]] = sums

    spread(row_ref[pl.ds(t, 1), :], q, quot_rows, val, store)


def quot_grads(first, count, got, rtab, quot_rows, old=None):
    sources, _, width = got.shape
    tables, rem_rows, _ = rtab.shape
    slots = sources * CAP
    rtab = pltpu.with_memory_space_constraint(rtab, pltpu.HBM)
    ins, extra, alias = [got, got, rtab], [], {}
    if old is not None:
        ins.append(old)
        extra = [pl.BlockSpec(memory_space=pltpu.HBM)]
        alias = {3: 0}
    return pl.pallas_call(
        functools.partial(quot_kernel, first, tables),
        out_shape=jax.ShapeDtypeStruct((tables, quot_rows, width), f32),
        grid=(count,),
        in_specs=[
            pl.BlockSpec((sources, CAP, width), lambda t: (0, first + t, 0)),
            pl.BlockSpec((sources, KEY_ROWS, width), lambda t: (0, tables * CAP // KEY_ROWS, 0)),
            pl.BlockSpec((1, rem_rows, width), lambda t: (first + t, 0, 0)),
        ]
        + extra,
        out_specs=pl.BlockSpec((1, quot_rows, width), lambda t: (first + t, 0, 0)),
        scratch_shapes=[pltpu.VMEM((slots, width), bf), pltpu.VMEM((width, slots), f32)],
        input_output_aliases=alias,
        cost_estimate=pl.CostEstimate(
            flops=count * 4 * slots * rem_rows * width, bytes_accessed=1 << 23, transcendentals=0
        ),
        compiler_params=pltpu.CompilerParams(vmem_limit_bytes=16 << 20),
        name="quot_grads",
    )(*ins)


def turn(a, s, flip):
    return lax.ppermute(a, CZY, turn_pairs(s, flip))


def add(*parts):
    total = parts[0].astype(f32)
    for p in parts[1:]:
        total = total + p.astype(f32)
    return total


def ring_scatter(low, high, flip):
    far_low = turn(low[2], 1, flip)
    near_low = turn(low[3], -1, flip)
    far_high = turn(high[2], -1, flip)
    near_high = turn(high[1], 1, flip)
    sum_low = turn(add(low[1], far_low).astype(bf), 1, flip)
    sum_high = turn(add(high[3], far_high).astype(bf), -1, flip)
    return add(low[0], near_low, sum_low), add(high[0], near_high, sum_high)


def ring_gather(low, high, flip):
    prev_low = turn(low, 1, flip)
    next_high = turn(high, -1, flip)
    next_low = turn(low, -1, flip)
    prev_high = turn(high, 1, flip)
    far_low = turn(prev_low, 1, flip)
    far_high = turn(next_high, -1, flip)
    return [low, next_low, far_low, prev_low], [high, next_high, far_high, prev_high]


def place_kernel(rels, where_ref, *refs):
    count = 2 * len(rels)
    ins = refs[:count]
    out_ref, buf, in_sem, out_sem = refs[-4:]
    half = out_ref.shape[0] // 2
    at = where_ref[1]

    def move(along_z):
        takes = [pltpu.make_async_copy(ins[i], buf.at[i], in_sem.at[i]) for i in range(count)]
        puts = []
        for i in range(count):
            far = (at + rels[i // 2]) % 4
            tabs = pl.ds(i % 2 * half, half)
            to = out_ref.at[tabs, far] if along_z else out_ref.at[tabs, :, far]
            puts.append(pltpu.make_async_copy(buf.at[i], to, out_sem.at[i]))
        for take in takes:
            take.start()
        for take, put in zip(takes, puts):
            take.wait()
            put.start()
        for put in puts:
            put.wait()

    pl.when(where_ref[0] == 0)(lambda: move(True))
    pl.when(where_ref[0] != 0)(lambda: move(False))


def place(rels, where, pieces, shape, old=None):
    ins = [x for lh in pieces for x in lh]
    count = len(ins)
    alias = {}
    if old is not None:
        ins.append(old)
        alias = {len(ins): 0}
    hbm = pl.BlockSpec(memory_space=pl.ANY)
    return pl.pallas_call(
        functools.partial(place_kernel, rels),
        out_shape=jax.ShapeDtypeStruct(shape, bf),
        grid_spec=pltpu.PrefetchScalarGridSpec(
            num_scalar_prefetch=1,
            grid=(),
            in_specs=[hbm] * len(ins),
            out_specs=hbm,
            scratch_shapes=[
                pltpu.VMEM((count,) + ins[0].shape, bf),
                pltpu.SemaphoreType.DMA((count,)),
                pltpu.SemaphoreType.DMA((count,)),
            ],
        ),
        input_output_aliases=alias,
        cost_estimate=pl.CostEstimate(flops=0, bytes_accessed=len(rels) << 21, transcendentals=0),
        compiler_params=pltpu.CompilerParams(vmem_limit_bytes=8 << 20),
        name="place",
    )(where, *ins)


def rank_sums(feat, cot, cross_in, cross_out):
    ci = lax.axis_index("c").astype(jnp.int32).reshape(1)
    xi = lax.axis_index("x").astype(jnp.int32).reshape(1)
    swap = lambda a: lax.ppermute(a, "c", [(0, 1), (1, 0)])
    got = swap(rank_part(1 - ci, feat, cot, cross_in, cross_out, bf))
    keep = rank_part(ci, feat, cot, cross_in, cross_out, f32)
    parts = mix(xi, keep, got)
    far = lax.ppermute(parts[2], "x", ring(NX, 2))
    nxt = lax.ppermute(parts[1], "x", ring(NX, 1))
    prev = lax.ppermute(parts[3], "x", ring(NX, 3))
    mine = add(parts[0], far, nxt, prev).astype(bf)
    far = lax.ppermute(mine, "x", ring(NX, 2))
    prev = lax.ppermute(mine, "x", ring(NX, 1))
    nxt = lax.ppermute(mine, "x", ring(NX, 3))
    own = (mine, prev, far, nxt)
    return own + tuple(swap(a) for a in own)


def update_kernel(own_ref, next_ref, far_ref, prev_ref, acc_ref, tab_ref, new_ref, out_ref):
    tables, subs, _, width = own_ref.shape
    accs = acc_ref[...].T
    lane = lax.broadcasted_iota(jnp.int32, accs.shape, 1)
    done = jnp.zeros_like(accs)
    for i in range(tables * subs):
        t, s = divmod(i, subs)
        grad = (own_ref[t, s].astype(f32) + far_ref[t, s].astype(f32)) + (
            next_ref[t, s].astype(f32) + prev_ref[t, s].astype(f32)
        )
        mean = jnp.sum(grad * grad, axis=1, keepdims=True) * (1.0 / width)
        acc = accs[:, i : i + 1] + mean
        new = tab_ref[t, s].astype(f32) - step_rate * grad * lax.rsqrt(acc + epsilon)
        new_ref[t, s] = new.astype(bf)
        done = jnp.where(lane == i, acc, done)
    out_ref[...] = done.T


def update(ring_parts, acc, tab):
    vmem = pl.BlockSpec(memory_space=pltpu.VMEM)
    tables, subs, rows, _ = tab.shape
    new, out = pl.pallas_call(
        update_kernel,
        out_shape=(
            jax.ShapeDtypeStruct(tab.shape, bf),
            jax.ShapeDtypeStruct((tables * subs, rows), f32),
        ),
        in_specs=[vmem] * 6,
        out_specs=(vmem, vmem),
        cost_estimate=pl.CostEstimate(flops=tab.size * 8, bytes_accessed=4 << 20, transcendentals=0),
        compiler_params=pltpu.CompilerParams(vmem_limit_bytes=12 << 20),
        name="update",
    )(*ring_parts, acc.reshape(tables * subs, rows), tab)
    return out.reshape(acc.shape), new


def device_step(
    features, cotangent, cross_in, cross_out, bias, dest_shard, quot_row, rem_row,
    quot_slab, quot_accum, rem_table, rem_accum,
):
    samples = features.shape[0]
    tables = quot_slab.shape[0]
    width = quot_slab.shape[2]
    rem_rows = rem_table.shape[1]
    rows = NZ * NY
    cap = CAP
    ci, zi, yi = lax.axis_index("c"), lax.axis_index("z"), lax.axis_index("y")

    target = dest_shard[:, :, 0]
    onehot = target[:, :, None] == jnp.arange(rows, dtype=jnp.int32)[None, None, :]
    lower = (
        jnp.arange(samples, dtype=jnp.int32)[:, None]
        >= jnp.arange(samples, dtype=jnp.int32)[None, :]
    ).astype(bf)
    running = jnp.einsum("ij,tjn->tin", lower, onehot.astype(bf), preferred_element_type=f32)
    slot_index = jnp.sum(jnp.where(onehot, running, 0.0), axis=2).astype(jnp.int32) - 1
    position = target * cap + slot_index
    digits = digit_lanes(quot_row, rem_row, width)

    pieces = rank_sums(features, cotangent, cross_in, cross_out)
    xi = lax.axis_index("x")
    send = pooled_dispatch(
        jnp.stack([ci, xi]).astype(jnp.int32), pieces, cotangent, cross_out, cross_in,
        bias.reshape(1, -1), position.reshape(tables, 1, samples), digits, rows, cap, width,
    )
    got = lax.all_to_all(send, ("z", "y"), split_axis=0, concat_axis=0, tiled=True)
    along_z = ci == 0
    at_one = jnp.where(along_z, zi, yi)
    at_two = jnp.where(along_z, yi, zi)
    where = jnp.stack([ci, at_one, at_one]).astype(jnp.int32)
    half = tables // 2
    low = rem_parts(0, half, where, got, quot_slab, rem_rows)
    high = rem_parts(half, half, where, got, quot_slab, rem_rows)

    one_low, one_high = ring_scatter(low, high, False)
    ring_low, ring_high = ring_gather(one_low.astype(bf), one_high.astype(bf), True)
    share = rem_rows // rows
    view = (tables, NZ, NY, share)

    def quarter(a):
        a = a.reshape(view + a.shape[2:])
        return jnp.where(
            along_z,
            lax.dynamic_index_in_dim(a, zi, 1, keepdims=False),
            lax.dynamic_index_in_dim(a, yi, 2, keepdims=False),
        )

    acc_in, tab_in = quarter(rem_accum), quarter(rem_table)
    acc_low, new_low = update(ring_low, acc_in[:half], tab_in[:half])
    acc_high, new_high = update(ring_high, acc_in[half:], tab_in[half:])
    acc = jnp.concatenate([acc_low, acc_high], axis=0)
    rem_acc_out = lax.dynamic_index_in_dim(acc, at_two, 1, keepdims=False)
    all_low, all_high = ring_gather(new_low, new_high, False)
    shape = (tables, NZ, NY, share, width)
    near = [(all_low[k], all_high[k]) for k in (0, 1, 3)]
    rem_out = place((0, 1, 3), where, near, shape)
    rem_out = place((2,), where, [(all_low[2], all_high[2])], shape, rem_out)
    rem_out = rem_out.reshape(tables, rem_rows, width)

    quot_rows = quot_slab.shape[1]
    quot_grad = quot_grads(0, half, got, rem_table, quot_rows)
    quot_grad = quot_grads(half, half, got, rem_table, quot_rows, quot_grad)
    quot_acc_out = quot_accum + jnp.mean(quot_grad * quot_grad, axis=-1)
    quot_out = (
        quot_slab.astype(f32)
        - step_rate * quot_grad * lax.rsqrt(quot_acc_out + epsilon)[..., None]
    ).astype(bf)
    return (quot_out, quot_acc_out, rem_out, rem_acc_out)


def solution(mesh):
    fine = Mesh(mesh.devices.reshape(NX, NC, NZ, NY), ("x", "c", "z", "y"))
    T, R = ("x", "c"), ("z", "y")
    return jax.shard_map(
        device_step,
        mesh=fine,
        in_specs=(
            P(R, T), P(R, T), P(T, None), P(T, None), P(T), P(T, R, None), P(T, R), P(T, R),
            P(T, R, None), P(T, R), P(T, None, None), P(T, None),
        ),
        out_specs=(P(T, R, None), P(T, R), P(T, None, None), P(T, R)),
        check_vma=False,
    )
```

```python
import functools

import jax
import jax.numpy as jnp
from jax import lax
from jax.experimental import pallas as pl
from jax.experimental.pallas import tpu as pltpu
from jax.sharding import Mesh
from jax.sharding import PartitionSpec as P


step_rate = 0.3
epsilon = 1e-06
bf = jnp.bfloat16
f32 = jnp.float32
NX, NC, NZ, NY = 4, 2, 4, 4
CZY = ("c", "z", "y")
NT = (((1,), (1,)), ((), ()))


def ring(n, s):
    return [(i, (i + s) % n) for i in range(n)]


def spot(c, z, y):
    return (c * NZ + z) * NY + y


def turn_pairs(s, flip):
    out = []
    for c in range(NC):
        for z in range(NZ):
            for y in range(NY):
                if (c == 0) != flip:
                    to = spot(c, (z + s) % NZ, y)
                else:
                    to = spot(c, z, (y + s) % NY)
                out.append((spot(c, z, y), to))
    return out


def rank_kernel(half_ref, feat_ref, cot_ref, ci_ref, co_ref, out_ref, acc_ref):
    step = pl.program_id(0)
    rank = ci_ref.shape[1]
    feat = feat_ref[...]
    product = (cot_ref[...].astype(f32) * feat.astype(f32)).astype(bf)

    @pl.when(step == 0)
    def _():
        acc_ref[...] = jnp.zeros_like(acc_ref)

    acc_ref[:, :rank] += jnp.dot(feat, ci_ref[...], preferred_element_type=f32)
    acc_ref[:, rank:] += jnp.dot(product, co_ref[...], preferred_element_type=f32)

    @pl.when(step == pl.num_programs(0) - 1)
    def _():
        out_ref[...] = acc_ref[...].astype(out_ref.dtype)


def rank_part(half, feat, cot, ci, co, dtype):
    size = feat.shape[0] // NC
    depth, rank = ci.shape
    feat, cot, ci, co = (
        pltpu.with_memory_space_constraint(a, pltpu.HBM) for a in (feat, cot, ci, co)
    )
    tile = depth // 4
    return pl.pallas_call(
        rank_kernel,
        out_shape=jax.ShapeDtypeStruct((size, 2 * rank), dtype),
        grid_spec=pltpu.PrefetchScalarGridSpec(
            num_scalar_prefetch=1,
            grid=(depth // tile,),
            in_specs=[
                pl.BlockSpec((size, tile), lambda k, h: (h[0], k)),
                pl.BlockSpec((size, tile), lambda k, h: (h[0], k)),
                pl.BlockSpec((tile, rank), lambda k, h: (k, 0)),
                pl.BlockSpec((tile, rank), lambda k, h: (k, 0)),
            ],
            out_specs=pl.BlockSpec((size, 2 * rank), lambda k, h: (0, 0)),
            scratch_shapes=[pltpu.VMEM((size, 2 * rank), f32)],
        ),
        cost_estimate=pl.CostEstimate(
            flops=4 * size * depth * rank, bytes_accessed=4 << 20, transcendentals=0
        ),
        compiler_params=pltpu.CompilerParams(vmem_limit_bytes=12 << 20),
        name="rank_part",
    )(half, feat, cot, ci, co)


def mix_kernel(x_ref, keep_ref, got_ref, *outs):
    size = outs[0].shape[0]
    for k, out in enumerate(outs):
        at = pl.ds(pl.multiple_of((x_ref[0] + k) % NX * size, size), size)
        out[...] = (keep_ref[at, :] + got_ref[at, :].astype(f32)).astype(bf)


def mix(xi, keep, got):
    piece = jax.ShapeDtypeStruct((keep.shape[0] // NX, keep.shape[1]), bf)
    vmem = pl.BlockSpec(memory_space=pltpu.VMEM)
    return pl.pallas_call(
        mix_kernel,
        out_shape=(piece,) * NX,
        grid_spec=pltpu.PrefetchScalarGridSpec(
            num_scalar_prefetch=1, grid=(), in_specs=[vmem] * 2, out_specs=[vmem] * NX
        ),
        compiler_params=pltpu.CompilerParams(vmem_limit_bytes=8 << 20),
        name="mix",
    )(xi, keep, got)


def pooled_kernel(at_ref, *refs):
    pieces, (cot_ref, co_ref, ci_ref, bias_ref, pos_ref, dig_ref, out_ref, key_ref, rank_ref) = (
        refs[: NC * NX],
        refs[NC * NX :],
    )
    rank = co_ref.shape[1]
    width, cap = key_ref.shape[1], CAP

    @pl.when(pl.program_id(0) == 0)
    def _():
        size = pieces[0].shape[0]
        for i, piece in enumerate(pieces):
            c = at_ref[0] if i < NX else 1 - at_ref[0]
            row = (c * NX + (at_ref[1] + NX - i % NX) % NX) * size
            rank_ref[pl.ds(pl.multiple_of(row, size), size), :] = piece[...]

    dests = out_ref.shape[0]
    tables = (out_ref.shape[1] - KEY_ROWS) // cap
    samples = cot_ref.shape[0]
    here = pos_ref.shape[0]
    step = pl.program_id(0)
    gate = (
        lax.dot_general(rank_ref[:, :rank], co_ref[...], NT, preferred_element_type=f32)
        + bias_ref[...]
    )
    back = lax.dot_general(rank_ref[:, rank:], ci_ref[...], NT, preferred_element_type=f32)
    pooled = (cot_ref[...].astype(f32) * (gate + 1.0) + back).astype(bf)
    slot = lax.broadcasted_iota(jnp.int32, (dests * cap, samples), 0)
    owner = lax.broadcasted_iota(jnp.int32, (samples, width), 1) % LANES // DIGITS
    keys = jnp.zeros((dests * cap, width), f32)
    for k in range(here):
        t = step * here + k
        placed = jnp.where(slot == pos_ref[k], 1.0, 0.0).astype(bf)
        digits = jnp.where(owner == t, dig_ref[...].astype(f32), 0.0).astype(bf)
        both = jnp.concatenate([pooled[:, k * width : (k + 1) * width], digits], axis=1)
        rows = jnp.dot(placed, both, preferred_element_type=f32)
        spot = pl.ds(pl.multiple_of(t * cap, KEY_ROWS), cap)
        out_ref[:, spot] = rows[:, :width].astype(bf).reshape(dests, cap, width)
        keys = keys + rows[:, width:]

    @pl.when(step == 0)
    def _():
        key_ref[...] = keys

    @pl.when(step > 0)
    def _():
        key_ref[...] += keys

    @pl.when(step == pl.num_programs(0) - 1)
    def _():
        parts = key_ref[...].reshape(dests, cap // KEY_ROWS, KEY_ROWS, width)
        group = lax.broadcasted_iota(jnp.int32, (dests, KEY_ROWS, width), 2) // LANES
        packed = jnp.zeros((dests, KEY_ROWS, width), f32)
        for k in range(cap // KEY_ROWS):
            packed = jnp.where(group == k, parts[:, k], packed)
        out_ref[:, tables * cap :] = packed.astype(bf)


def pooled_dispatch(where, pieces, cot, co, ci, bias, pos, digits, dests, cap, width):
    samples = cot.shape[0]
    tables = pos.shape[0]
    pair = 2
    out = (dests, tables * cap + KEY_ROWS, width)
    return pl.pallas_call(
        pooled_kernel,
        out_shape=pltpu.HBM(out, bf),
        grid_spec=pltpu.PrefetchScalarGridSpec(
            num_scalar_prefetch=1,
            grid=(tables // pair,),
            in_specs=[pl.BlockSpec(memory_space=pltpu.VMEM)] * len(pieces)
            + [
                pl.BlockSpec((samples, pair * width), lambda i, w: (0, i)),
                pl.BlockSpec((pair * width, co.shape[1]), lambda i, w: (i, 0)),
                pl.BlockSpec((pair * width, co.shape[1]), lambda i, w: (i, 0)),
                pl.BlockSpec((1, pair * width), lambda i, w: (0, i)),
                pl.BlockSpec((pair, 1, samples), lambda i, w: (i, 0, 0)),
                pl.BlockSpec(digits.shape, lambda i, w: (0, 0)),
            ],
            out_specs=pl.BlockSpec(out, lambda i, w: (0, 0, 0)),
            scratch_shapes=[
                pltpu.VMEM((dests * cap, width), f32),
                pltpu.VMEM((samples, pieces[0].shape[1]), bf),
            ],
        ),
        compiler_params=pltpu.CompilerParams(vmem_limit_bytes=12 << 20),
        name="pooled_dispatch",
    )(where, *pieces, cot, co, ci, bias, pos, digits)


DIGITS, QB, MB, LANES, KEY_ROWS, CAP = 4, 32, 64, 32, 16, 48
PARTS = 2


def digit_lanes(q, m, width):
    parts = jnp.stack([q // QB, q % QB, m // MB, m % MB], axis=1)
    parts = parts.reshape(-1, q.shape[1])
    parts = jnp.concatenate([parts] * (CAP // KEY_ROWS), axis=0)
    parts = jnp.pad(parts, ((0, width - parts.shape[0]), (0, 0)))
    return parts.T.astype(bf)


def unpack_keys(packed):
    sources, _, width = packed.shape
    group = lax.broadcasted_iota(jnp.int32, packed.shape, 2) // LANES
    packed = packed.astype(f32)
    parts = [jnp.where(group == k, packed, 0.0)[:, None] for k in range(CAP // KEY_ROWS)]
    return jnp.concatenate(parts, axis=1).reshape(sources * CAP, width).astype(bf)


def key_rows(keys, tables):
    width = keys.shape[1]
    lane = lax.broadcasted_iota(jnp.int32, (width, width), 0) % LANES
    col = lax.broadcasted_iota(jnp.int32, (width, width), 1)
    t = col % tables
    base = DIGITS * t + jnp.where(col >= tables, 2, 0)
    high = jnp.where(col >= tables, MB, QB).astype(f32)
    comb = jnp.where(lane == base, high, jnp.where(lane == base + 1, 1.0, 0.0))
    comb = jnp.where(col < 2 * tables, comb, 0.0).astype(bf)
    return jnp.dot(keys, comb, preferred_element_type=f32).T


def key_lanes(keys, t):
    width = keys.shape[1]
    lane = lax.broadcasted_iota(jnp.int32, (width, 2 * width), 0) % LANES - DIGITS * t
    side = lax.broadcasted_iota(jnp.int32, (width, 2 * width), 1) >= width
    lane = jnp.where(side, lane - 2, lane)
    high = jnp.where(side, float(MB), float(QB))
    comb = jnp.where(lane == 0, high, jnp.where(lane == 1, 1.0, 0.0)).astype(bf)
    out = jnp.dot(keys, comb, preferred_element_type=f32)
    return out[:, :width], out[:, width:]


def pick(key, tab):
    slots, width = key.shape
    half = tab.shape[0] // 2
    both = jnp.concatenate([tab[:half], tab[half:]], axis=1)
    size = slots // PARTS
    out = []
    for p in range(PARTS):
        part = key[p * size : (p + 1) * size]
        high = part >= half
        low = jnp.where(high, part - half, part)
        lane = lax.broadcasted_iota(jnp.int32, (size, width), 1).astype(f32)
        hot = jnp.concatenate(
            [jnp.where(low - j == lane, 1.0, 0.0).astype(bf) for j in range(0, half, width)],
            axis=1,
        )
        got = jnp.dot(hot, both, preferred_element_type=f32)
        out.append(jnp.where(high, got[:, width:], got[:, :width]))
    return jnp.concatenate(out, axis=0)


def spread(row, key, rows, val, store):
    slots = row.shape[1]
    width = val.shape[1]
    half = rows // 2
    low = jnp.where(row >= half, row - half, row)
    high = key >= half
    both = jnp.concatenate(
        [jnp.where(high, 0.0, val).astype(bf), jnp.where(high, val, 0.0).astype(bf)], axis=1
    )
    size = half // PARTS
    at = lax.broadcasted_iota(jnp.int32, (size, slots), 0).astype(f32)
    for p in range(PARTS):
        hot = jnp.where(at == low - p * size, 1.0, 0.0).astype(bf)
        sums = jnp.dot(hot, both, preferred_element_type=f32)
        store(p * size, sums[:, :width])
        store(half + p * size, sums[:, width:])


def rem_kernel(
    first, tables, where_ref, got_ref, slab_ref, r0, r1, r2, r3,
    g_buf, pack_buf, slab_buf, sum_ref, sem, pack_sem,
):
    count, sources, cap, width = g_buf.shape
    slots = sources * cap
    rem_rows = sum_ref.shape[0]
    pack = pltpu.make_async_copy(
        got_ref.at[:, pl.ds(tables * cap, KEY_ROWS)], pack_buf, pack_sem
    )
    pack.start()

    def inputs(k):
        return (
            pltpu.make_async_copy(
                got_ref.at[:, pl.ds((first + k) * cap, cap)], g_buf.at[k], sem.at[0, k]
            ),
            pltpu.make_async_copy(slab_ref.at[first + k], slab_buf.at[k], sem.at[1, k]),
        )

    copies = [inputs(k) for k in range(count)]
    for pair in copies:
        for copy in pair:
            copy.start()
    pack.wait()
    keys = unpack_keys(pack_buf[...])
    rows = key_rows(keys, tables)
    sub_rows = r0.shape[2]
    at = where_ref[1]
    along_z = where_ref[0] == 0
    for k in range(count):
        for copy in copies[k]:
            copy.wait()
        t = first + k
        g = g_buf[k].reshape(slots, width).astype(f32)
        q, m = key_lanes(keys, t)
        val = g * pick(q, slab_buf[k])


        def store(at, sums):
            sum_ref[at : at + sums.shape[0]] = sums.astype(bf)

        spread(rows[tables + t : tables + t + 1], m, rem_rows, val, store)
        for rel, ref in enumerate((r0, r1, r2, r3)):
            far = (at + rel) % 4
            for sub in range(4):
                block = jnp.where(along_z, far * NY + sub, sub * NY + far)
                start = pl.multiple_of(block * sub_rows, sub_rows)
                ref[k, sub] = sum_ref[pl.ds(start, sub_rows), :]


def rem_parts(first, count, where, got, slab, rem_rows):
    sources, _, width = got.shape
    tables, quot_rows, _ = slab.shape
    slots = sources * CAP
    slab = pltpu.with_memory_space_constraint(slab, pltpu.HBM)
    sub = rem_rows // (NZ * NY)
    piece = jax.ShapeDtypeStruct((count, 4, sub, width), bf)
    return pl.pallas_call(
        functools.partial(rem_kernel, first, tables),
        out_shape=(piece,) * 4,
        grid_spec=pltpu.PrefetchScalarGridSpec(
            num_scalar_prefetch=1,
            grid=(),
            in_specs=[
                pl.BlockSpec(memory_space=pl.ANY),
                pl.BlockSpec(memory_space=pltpu.HBM),
            ],
            out_specs=[pl.BlockSpec(memory_space=pltpu.VMEM)] * 4,
            scratch_shapes=[
                pltpu.VMEM((count, sources, CAP, width), bf),
                pltpu.VMEM((sources, KEY_ROWS, width), bf),
                pltpu.VMEM((count, quot_rows, width), bf),
                pltpu.VMEM((rem_rows, width), bf),
                pltpu.SemaphoreType.DMA((2, count)),
                pltpu.SemaphoreType.DMA,
            ],
        ),
        cost_estimate=pl.CostEstimate(
            flops=count * 4 * slots * rem_rows * width, bytes_accessed=1 << 22, transcendentals=0
        ),
        compiler_params=pltpu.CompilerParams(vmem_limit_bytes=12 << 20),
        name="rem_parts",
    )(where, got, slab)


def lane_mean(x):
    width = x.shape[1]
    square = x * x
    high = square.astype(bf)
    low = (square - high.astype(f32)).astype(bf)
    ones = jnp.full((width, width), 1.0 / width, bf)
    return jnp.dot(high, ones, preferred_element_type=f32) + jnp.dot(
        low, ones, preferred_element_type=f32
    )


def quot_kernel(first, tables, g_ref, pack_ref, rtab_ref, slab_ref, acc_ref, *refs):
    quot_ref, out_ref, key_ref, row_ref, sum_ref, col_ref, done_ref = refs[-7:]
    sources, cap, width = g_ref.shape
    slots = sources * cap
    quot_rows = quot_ref.shape[1]
    step = pl.program_id(0)
    t = first + step

    @pl.when(step == 0)
    def _():
        keys = unpack_keys(pack_ref[...])
        key_ref[...] = keys
        row_ref[...] = key_rows(keys, tables)
        col_ref[...] = acc_ref[...].T

    g = g_ref[...].reshape(slots, width).astype(f32)
    q, m = key_lanes(key_ref[...], t)
    val = g * pick(m, rtab_ref[0])

    def store(at, sums):
        sum_ref[at : at + sums.shape[0]] = sums

    spread(row_ref[pl.ds(t, 1), :], q, quot_rows, val, store)
    size = quot_rows // 4
    for at in range(0, quot_rows, size):
        part = slice(at, at + size)
        grad = sum_ref[part]
        col = lax.broadcasted_iota(jnp.int32, (size, tables), 1)
        old = jnp.sum(jnp.where(col == t, col_ref[part], 0.0), axis=1, keepdims=True)
        acc = old + lane_mean(grad)
        new = slab_ref[0, part].astype(f32) - step_rate * grad * lax.rsqrt(acc + epsilon)
        quot_ref[0, part] = new.astype(bf)
        lane = lax.broadcasted_iota(jnp.int32, (size, width), 1)
        done_ref[part] = jnp.where(lane == step, acc, done_ref[part])

    @pl.when(step == pl.num_programs(0) - 1)
    def _():
        out_ref[...] = done_ref[...].T[: out_ref.shape[0]]


def quot_update(first, count, got, rtab, slab, accum, old=None):
    sources, _, width = got.shape
    tables, rem_rows, _ = rtab.shape
    quot_rows = slab.shape[1]
    slots = sources * CAP
    rtab = pltpu.with_memory_space_constraint(rtab, pltpu.HBM)
    slab = pltpu.with_memory_space_constraint(slab, pltpu.HBM)
    ins, extra, alias = [got, got, rtab, slab, accum], [], {}
    if old is not None:
        ins.append(old)
        extra = [pl.BlockSpec(memory_space=pltpu.HBM)]
        alias = {len(ins) - 1: 0}
    return pl.pallas_call(
        functools.partial(quot_kernel, first, tables),
        out_shape=(
            pltpu.HBM(slab.shape, bf),
            jax.ShapeDtypeStruct((tables, quot_rows), f32),
        ),
        grid=(count,),
        in_specs=[
            pl.BlockSpec((sources, CAP, width), lambda t: (0, first + t, 0)),
            pl.BlockSpec((sources, KEY_ROWS, width), lambda t: (0, tables * CAP // KEY_ROWS, 0)),
            pl.BlockSpec((1, rem_rows, width), lambda t: (first + t, 0, 0)),
            pl.BlockSpec((1, quot_rows, width), lambda t: (first + t, 0, 0)),
            pl.BlockSpec((tables, quot_rows), lambda t: (0, 0)),
        ]
        + extra,
        out_specs=(
            pl.BlockSpec((1, quot_rows, width), lambda t: (first + t, 0, 0)),
            pl.BlockSpec((tables, quot_rows), lambda t: (0, 0)),
        ),
        scratch_shapes=[
            pltpu.VMEM((slots, width), bf),
            pltpu.VMEM((width, slots), f32),
            pltpu.VMEM((quot_rows, width), f32),
            pltpu.VMEM((quot_rows, tables), f32),
            pltpu.VMEM((quot_rows, width), f32),
        ],
        input_output_aliases=alias,
        cost_estimate=pl.CostEstimate(
            flops=count * 4 * slots * rem_rows * width, bytes_accessed=1 << 23, transcendentals=0
        ),
        compiler_params=pltpu.CompilerParams(vmem_limit_bytes=14 << 20),
        name="quot_update",
    )(*ins)


def turn(a, s, flip):
    return lax.ppermute(a, CZY, turn_pairs(s, flip))


def add(*parts):
    total = parts[0].astype(f32)
    for p in parts[1:]:
        total = total + p.astype(f32)
    return total


def ring_scatter(low, high, flip):
    far_low = turn(low[2], 1, flip)
    near_low = turn(low[3], -1, flip)
    far_high = turn(high[2], -1, flip)
    near_high = turn(high[1], 1, flip)
    sum_low = turn(add(low[1], far_low).astype(bf), 1, flip)
    sum_high = turn(add(high[3], far_high).astype(bf), -1, flip)
    return add(low[0], near_low, sum_low), add(high[0], near_high, sum_high)


def ring_gather(low, high, flip):
    prev_low = turn(low, 1, flip)
    next_high = turn(high, -1, flip)
    next_low = turn(low, -1, flip)
    prev_high = turn(high, 1, flip)
    far_low = turn(prev_low, 1, flip)
    far_high = turn(next_high, -1, flip)
    return [low, next_low, far_low, prev_low], [high, next_high, far_high, prev_high]


def place_kernel(rels, where_ref, *refs):
    count = 2 * len(rels)
    ins = refs[:count]
    out_ref, buf, in_sem, out_sem = refs[-4:]
    half = out_ref.shape[0] // 2
    at = where_ref[1]

    def move(along_z):
        takes = [pltpu.make_async_copy(ins[i], buf.at[i], in_sem.at[i]) for i in range(count)]
        puts = []
        for i in range(count):
            far = (at + rels[i // 2]) % 4
            tabs = pl.ds(i % 2 * half, half)
            to = out_ref.at[tabs, far] if along_z else out_ref.at[tabs, :, far]
            puts.append(pltpu.make_async_copy(buf.at[i], to, out_sem.at[i]))
        for take in takes:
            take.start()
        for take, put in zip(takes, puts):
            take.wait()
            put.start()
        for put in puts:
            put.wait()

    pl.when(where_ref[0] == 0)(lambda: move(True))
    pl.when(where_ref[0] != 0)(lambda: move(False))


def place(rels, where, pieces, shape, old=None):
    ins = [x for lh in pieces for x in lh]
    count = len(ins)
    alias = {}
    if old is not None:
        ins.append(old)
        alias = {len(ins): 0}
    hbm = pl.BlockSpec(memory_space=pl.ANY)
    return pl.pallas_call(
        functools.partial(place_kernel, rels),
        out_shape=jax.ShapeDtypeStruct(shape, bf),
        grid_spec=pltpu.PrefetchScalarGridSpec(
            num_scalar_prefetch=1,
            grid=(),
            in_specs=[hbm] * len(ins),
            out_specs=hbm,
            scratch_shapes=[
                pltpu.VMEM((count,) + ins[0].shape, bf),
                pltpu.SemaphoreType.DMA((count,)),
                pltpu.SemaphoreType.DMA((count,)),
            ],
        ),
        input_output_aliases=alias,
        cost_estimate=pl.CostEstimate(flops=0, bytes_accessed=len(rels) << 21, transcendentals=0),
        compiler_params=pltpu.CompilerParams(vmem_limit_bytes=8 << 20),
        name="place",
    )(where, *ins)


def rank_sums(feat, cot, cross_in, cross_out, ready):
    ci = lax.axis_index("c").astype(jnp.int32).reshape(1)
    xi = lax.axis_index("x").astype(jnp.int32).reshape(1)
    swap = lambda a: lax.ppermute(a, "c", [(0, 1), (1, 0)])
    got = swap(rank_part(1 - ci, feat, cot, cross_in, cross_out, bf))
    keep = rank_part(ci, feat, cot, cross_in, cross_out, f32)
    parts = mix(xi, keep, got)
    far = lax.ppermute(parts[2], "x", ring(NX, 2))
    nxt = lax.ppermute(parts[1], "x", ring(NX, 1))
    prev = lax.ppermute(parts[3], "x", ring(NX, 3))
    mine = add(parts[0], far, nxt, prev).astype(bf)
    mine, ready = lax.optimization_barrier((mine, ready))
    far = lax.ppermute(mine, "x", ring(NX, 2))
    prev = lax.ppermute(mine, "x", ring(NX, 1))
    nxt = lax.ppermute(mine, "x", ring(NX, 3))
    own = (mine, prev, far, nxt)
    return own + tuple(swap(a) for a in own), ready


def update_kernel(own_ref, next_ref, far_ref, prev_ref, acc_ref, tab_ref, new_ref, out_ref):
    tables, subs, rows, width = own_ref.shape
    accs = acc_ref[...].T
    lane = lax.broadcasted_iota(jnp.int32, (rows, width), 1)
    done = jnp.zeros((rows, width), f32)
    for i in range(tables * subs):
        t, s = divmod(i, subs)
        grad = (own_ref[t, s].astype(f32) + far_ref[t, s].astype(f32)) + (
            next_ref[t, s].astype(f32) + prev_ref[t, s].astype(f32)
        )
        acc = accs[:, i : i + 1] + lane_mean(grad)
        new = tab_ref[t, s].astype(f32) - step_rate * grad * lax.rsqrt(acc + epsilon)
        new_ref[t, s] = new.astype(bf)
        done = jnp.where(lane == i, acc, done)
    out_ref[...] = done.T[: tables * subs]


def update(ring_parts, acc, tab):
    vmem = pl.BlockSpec(memory_space=pltpu.VMEM)
    tables, subs, rows, _ = tab.shape
    new, out = pl.pallas_call(
        update_kernel,
        out_shape=(
            jax.ShapeDtypeStruct(tab.shape, bf),
            jax.ShapeDtypeStruct((tables * subs, rows), f32),
        ),
        in_specs=[vmem] * 6,
        out_specs=(vmem, vmem),
        cost_estimate=pl.CostEstimate(flops=tab.size * 8, bytes_accessed=4 << 20, transcendentals=0),
        compiler_params=pltpu.CompilerParams(vmem_limit_bytes=12 << 20),
        name="update",
    )(*ring_parts, acc.reshape(tables * subs, rows), tab)
    return out.reshape(acc.shape), new


def device_step(
    features, cotangent, cross_in, cross_out, bias, dest_shard, quot_row, rem_row,
    quot_slab, quot_accum, rem_table, rem_accum,
):
    samples = features.shape[0]
    tables = quot_slab.shape[0]
    width = quot_slab.shape[2]
    rem_rows = rem_table.shape[1]
    rows = NZ * NY
    cap = CAP
    ci, zi, yi = lax.axis_index("c"), lax.axis_index("z"), lax.axis_index("y")

    target = dest_shard[:, :, 0]
    onehot = target[:, :, None] == jnp.arange(rows, dtype=jnp.int32)[None, None, :]
    lower = (
        jnp.arange(samples, dtype=jnp.int32)[:, None]
        >= jnp.arange(samples, dtype=jnp.int32)[None, :]
    ).astype(bf)
    running = jnp.einsum("ij,tjn->tin", lower, onehot.astype(bf), preferred_element_type=f32)
    slot_index = jnp.sum(jnp.where(onehot, running, 0.0), axis=2).astype(jnp.int32) - 1
    position = target * cap + slot_index
    digits = digit_lanes(quot_row, rem_row, width)

    position = position.reshape(tables, 1, samples)
    pieces, (position, digits) = rank_sums(
        features, cotangent, cross_in, cross_out, (position, digits)
    )
    xi = lax.axis_index("x")
    send = pooled_dispatch(
        jnp.stack([ci, xi]).astype(jnp.int32), pieces, cotangent, cross_out, cross_in,
        bias.reshape(1, -1), position, digits, rows, cap, width,
    )
    got = lax.all_to_all(send, ("z", "y"), split_axis=0, concat_axis=0, tiled=True)
    along_z = ci == 0
    at_one = jnp.where(along_z, zi, yi)
    at_two = jnp.where(along_z, yi, zi)
    where = jnp.stack([ci, at_one, at_one]).astype(jnp.int32)
    half = tables // 2
    low = rem_parts(0, half, where, got, quot_slab, rem_rows)
    high = rem_parts(half, half, where, got, quot_slab, rem_rows)

    one_low, one_high = ring_scatter(low, high, False)
    ring_low, ring_high = ring_gather(one_low.astype(bf), one_high.astype(bf), True)
    share = rem_rows // rows
    view = (tables, NZ, NY, share)

    def quarter(a):
        a = a.reshape(view + a.shape[2:])
        return jnp.where(
            along_z,
            lax.dynamic_index_in_dim(a, zi, 1, keepdims=False),
            lax.dynamic_index_in_dim(a, yi, 2, keepdims=False),
        )

    acc_in, tab_in = quarter(rem_accum), quarter(rem_table)
    acc_low, new_low = update(ring_low, acc_in[:half], tab_in[:half])
    acc_high, new_high = update(ring_high, acc_in[half:], tab_in[half:])
    acc = jnp.concatenate([acc_low, acc_high], axis=0)
    rem_acc_out = lax.dynamic_index_in_dim(acc, at_two, 1, keepdims=False)
    all_low, all_high = ring_gather(new_low, new_high, False)
    shape = (tables, NZ, NY, share, width)
    near = [(all_low[k], all_high[k]) for k in (0, 1, 3)]
    rem_out = place((0, 1, 3), where, near, shape)
    rem_out = place((2,), where, [(all_low[2], all_high[2])], shape, rem_out)
    rem_out = rem_out.reshape(tables, rem_rows, width)

    quot_out, acc_low = quot_update(0, half, got, rem_table, quot_slab, quot_accum)
    quot_out, acc_high = quot_update(half, half, got, rem_table, quot_slab, quot_accum, quot_out)
    quot_acc_out = jnp.concatenate([acc_low[:half], acc_high[:half]], axis=0)
    return (quot_out, quot_acc_out, rem_out, rem_acc_out)


def solution(mesh):
    fine = Mesh(mesh.devices.reshape(NX, NC, NZ, NY), ("x", "c", "z", "y"))
    T, R = ("x", "c"), ("z", "y")
    return jax.shard_map(
        device_step,
        mesh=fine,
        in_specs=(
            P(R, T), P(R, T), P(T, None), P(T, None), P(T), P(T, R, None), P(T, R), P(T, R),
            P(T, R, None), P(T, R), P(T, None, None), P(T, None),
        ),
        out_specs=(P(T, R, None), P(T, R), P(T, None, None), P(T, R)),
        check_vma=False,
    )
```

```python
import functools

import jax
import jax.numpy as jnp
from jax import lax
from jax.experimental import pallas as pl
from jax.experimental.pallas import tpu as pltpu
from jax.sharding import Mesh
from jax.sharding import PartitionSpec as P


step_rate = 0.3
epsilon = 1e-06
bf = jnp.bfloat16
f32 = jnp.float32
NX, NC, NZ, NY = 4, 2, 4, 4
CZY = ("c", "z", "y")
NT = (((1,), (1,)), ((), ()))


def ring(n, s):
    return [(i, (i + s) % n) for i in range(n)]


def spot(c, z, y):
    return (c * NZ + z) * NY + y


def turn_pairs(s, flip):
    out = []
    for c in range(NC):
        for z in range(NZ):
            for y in range(NY):
                if (c == 0) != flip:
                    to = spot(c, (z + s) % NZ, y)
                else:
                    to = spot(c, z, (y + s) % NY)
                out.append((spot(c, z, y), to))
    return out


def rank_kernel(at_ref, feat_ref, cot_ref, ci_ref, co_ref, *refs):
    outs, (feat_buf, cot_buf, ci_buf, co_buf, acc_ref, sem) = refs[: 2 * NX], refs[2 * NX :]
    chunks, samples, tile = feat_buf.shape
    rank = ci_ref.shape[1]

    def loads(k):
        at = pl.ds(k * tile, tile)
        return (
            pltpu.make_async_copy(feat_ref.at[:, at], feat_buf.at[k], sem.at[0, k]),
            pltpu.make_async_copy(ci_ref.at[at], ci_buf.at[k], sem.at[1, k]),
            pltpu.make_async_copy(cot_ref.at[:, at], cot_buf.at[k], sem.at[2, k]),
            pltpu.make_async_copy(co_ref.at[at], co_buf.at[k], sem.at[3, k]),
        )

    copies = [loads(k) for k in range(chunks)]
    for four in copies:
        for copy in four:
            copy.start()
    for k in range(chunks):
        for copy in copies[k]:
            copy.wait()
        feat = feat_buf[k]
        product = (cot_buf[k].astype(f32) * feat.astype(f32)).astype(bf)
        left = jnp.dot(feat, ci_buf[k], preferred_element_type=f32)
        right = jnp.dot(product, co_buf[k], preferred_element_type=f32)
        if k:
            acc_ref[:, :rank] += left
            acc_ref[:, rank:] += right
        else:
            acc_ref[:, :rank] = left
            acc_ref[:, rank:] = right
    size = samples // (NC * NX)
    for i, out in enumerate(outs):
        c = at_ref[0] if i >= NX else 1 - at_ref[0]
        row = (c * NX + (at_ref[1] + i % NX) % NX) * size
        out[...] = acc_ref[pl.ds(pl.multiple_of(row, size), size), :].astype(out.dtype)


def rank_parts(where, feat, cot, cross_in, cross_out):
    samples, depth = feat.shape
    rank = cross_in.shape[1]
    chunks = 2
    tile = depth // chunks
    ins = [
        pltpu.with_memory_space_constraint(a, pltpu.HBM)
        for a in (feat, cot, cross_in, cross_out)
    ]
    shape = (samples // (NC * NX), 2 * rank)
    return pl.pallas_call(
        rank_kernel,
        out_shape=(jax.ShapeDtypeStruct(shape, bf),) * NX
        + (jax.ShapeDtypeStruct(shape, f32),) * NX,
        grid_spec=pltpu.PrefetchScalarGridSpec(
            num_scalar_prefetch=1,
            grid=(),
            in_specs=[pl.BlockSpec(memory_space=pltpu.HBM)] * 4,
            out_specs=[pl.BlockSpec(memory_space=pltpu.VMEM)] * (2 * NX),
            scratch_shapes=[
                pltpu.VMEM((chunks, samples, tile), bf),
                pltpu.VMEM((chunks, samples, tile), bf),
                pltpu.VMEM((chunks, tile, rank), bf),
                pltpu.VMEM((chunks, tile, rank), bf),
                pltpu.VMEM((samples, 2 * rank), f32),
                pltpu.SemaphoreType.DMA((4, chunks)),
            ],
        ),
        cost_estimate=pl.CostEstimate(
            flops=4 * samples * depth * rank, bytes_accessed=8 << 20, transcendentals=0
        ),
        compiler_params=pltpu.CompilerParams(vmem_limit_bytes=16 << 20),
        name="rank_parts",
    )(where, *ins)


def pooled_kernel(at_ref, *refs):
    pieces, (cot_ref, co_ref, ci_ref, bias_ref, pos_ref, dig_ref, out_ref, key_ref, rank_ref) = (
        refs[: NC * NX],
        refs[NC * NX :],
    )
    rank = co_ref.shape[1]
    width, cap = key_ref.shape[1], CAP

    @pl.when(pl.program_id(0) == 0)
    def _():
        size = pieces[0].shape[0]
        for i, piece in enumerate(pieces):
            c = at_ref[0] if i < NX else 1 - at_ref[0]
            row = (c * NX + (at_ref[1] + NX - i % NX) % NX) * size
            rank_ref[pl.ds(pl.multiple_of(row, size), size), :] = piece[...]

    dests = out_ref.shape[0]
    tables = (out_ref.shape[1] - KEY_ROWS) // cap
    samples = cot_ref.shape[0]
    here = pos_ref.shape[0]
    step = pl.program_id(0)
    gate = (
        lax.dot_general(rank_ref[:, :rank], co_ref[...], NT, preferred_element_type=f32)
        + bias_ref[...]
    )
    back = lax.dot_general(rank_ref[:, rank:], ci_ref[...], NT, preferred_element_type=f32)
    pooled = (cot_ref[...].astype(f32) * (gate + 1.0) + back).astype(bf)
    slot = lax.broadcasted_iota(jnp.int32, (dests * cap, samples), 0)
    owner = lax.broadcasted_iota(jnp.int32, (samples, width), 1) % LANES // DIGITS
    keys = jnp.zeros((dests * cap, width), f32)
    for k in range(here):
        t = step * here + k
        placed = jnp.where(slot == pos_ref[k], 1.0, 0.0).astype(bf)
        digits = jnp.where(owner == t, dig_ref[...].astype(f32), 0.0).astype(bf)
        both = jnp.concatenate([pooled[:, k * width : (k + 1) * width], digits], axis=1)
        rows = jnp.dot(placed, both, preferred_element_type=f32)
        spot = pl.ds(pl.multiple_of(t * cap, KEY_ROWS), cap)
        out_ref[:, spot] = rows[:, :width].astype(bf).reshape(dests, cap, width)
        keys = keys + rows[:, width:]

    @pl.when(step == 0)
    def _():
        key_ref[...] = keys

    @pl.when(step > 0)
    def _():
        key_ref[...] += keys

    @pl.when(step == pl.num_programs(0) - 1)
    def _():
        parts = key_ref[...].reshape(dests, cap // KEY_ROWS, KEY_ROWS, width)
        group = lax.broadcasted_iota(jnp.int32, (dests, KEY_ROWS, width), 2) // LANES
        packed = jnp.zeros((dests, KEY_ROWS, width), f32)
        for k in range(cap // KEY_ROWS):
            packed = jnp.where(group == k, parts[:, k], packed)
        out_ref[:, tables * cap :] = packed.astype(bf)


def pooled_dispatch(where, pieces, cot, co, ci, bias, pos, digits, dests, cap, width):
    samples = cot.shape[0]
    tables = pos.shape[0]
    pair = 2
    out = (dests, tables * cap + KEY_ROWS, width)
    return pl.pallas_call(
        pooled_kernel,
        out_shape=pltpu.HBM(out, bf),
        grid_spec=pltpu.PrefetchScalarGridSpec(
            num_scalar_prefetch=1,
            grid=(tables // pair,),
            in_specs=[pl.BlockSpec(memory_space=pltpu.VMEM)] * len(pieces)
            + [
                pl.BlockSpec((samples, pair * width), lambda i, w: (0, i)),
                pl.BlockSpec((pair * width, co.shape[1]), lambda i, w: (i, 0)),
                pl.BlockSpec((pair * width, co.shape[1]), lambda i, w: (i, 0)),
                pl.BlockSpec((1, pair * width), lambda i, w: (0, i)),
                pl.BlockSpec((pair, 1, samples), lambda i, w: (i, 0, 0)),
                pl.BlockSpec(digits.shape, lambda i, w: (0, 0)),
            ],
            out_specs=pl.BlockSpec(out, lambda i, w: (0, 0, 0)),
            scratch_shapes=[
                pltpu.VMEM((dests * cap, width), f32),
                pltpu.VMEM((samples, pieces[0].shape[1]), bf),
            ],
        ),
        compiler_params=pltpu.CompilerParams(vmem_limit_bytes=12 << 20),
        name="pooled_dispatch",
    )(where, *pieces, cot, co, ci, bias, pos, digits)


DIGITS, QB, MB, LANES, KEY_ROWS, CAP = 4, 32, 64, 32, 16, 48
PARTS = 2


def digit_lanes(q, m, width):
    parts = jnp.stack([q // QB, q % QB, m // MB, m % MB], axis=1)
    parts = parts.reshape(-1, q.shape[1])
    parts = jnp.concatenate([parts] * (CAP // KEY_ROWS), axis=0)
    parts = jnp.pad(parts, ((0, width - parts.shape[0]), (0, 0)))
    return parts.T.astype(bf)


def unpack_keys(packed):
    sources, _, width = packed.shape
    group = lax.broadcasted_iota(jnp.int32, packed.shape, 2) // LANES
    packed = packed.astype(f32)
    parts = [jnp.where(group == k, packed, 0.0)[:, None] for k in range(CAP // KEY_ROWS)]
    return jnp.concatenate(parts, axis=1).reshape(sources * CAP, width).astype(bf)


def key_rows(keys, tables):
    width = keys.shape[1]
    lane = lax.broadcasted_iota(jnp.int32, (width, width), 0) % LANES
    col = lax.broadcasted_iota(jnp.int32, (width, width), 1)
    t = col % tables
    base = DIGITS * t + jnp.where(col >= tables, 2, 0)
    high = jnp.where(col >= tables, MB, QB).astype(f32)
    comb = jnp.where(lane == base, high, jnp.where(lane == base + 1, 1.0, 0.0))
    comb = jnp.where(col < 2 * tables, comb, 0.0).astype(bf)
    return jnp.dot(keys, comb, preferred_element_type=f32).T


def key_lanes(keys, t):
    width = keys.shape[1]
    lane = lax.broadcasted_iota(jnp.int32, (width, 2 * width), 0) % LANES - DIGITS * t
    side = lax.broadcasted_iota(jnp.int32, (width, 2 * width), 1) >= width
    lane = jnp.where(side, lane - 2, lane)
    high = jnp.where(side, float(MB), float(QB))
    comb = jnp.where(lane == 0, high, jnp.where(lane == 1, 1.0, 0.0)).astype(bf)
    out = jnp.dot(keys, comb, preferred_element_type=f32)
    return out[:, :width], out[:, width:]


def pick(key, tab):
    slots, width = key.shape
    half = tab.shape[0] // 2
    both = jnp.concatenate([tab[:half], tab[half:]], axis=1)
    size = slots // PARTS
    out = []
    for p in range(PARTS):
        part = key[p * size : (p + 1) * size]
        high = part >= half
        low = jnp.where(high, part - half, part)
        lane = lax.broadcasted_iota(jnp.int32, (size, width), 1).astype(f32)
        hot = jnp.concatenate(
            [jnp.where(low - j == lane, 1.0, 0.0).astype(bf) for j in range(0, half, width)],
            axis=1,
        )
        got = jnp.dot(hot, both, preferred_element_type=f32)
        out.append(jnp.where(high, got[:, width:], got[:, :width]))
    return jnp.concatenate(out, axis=0)


def spread(row, key, rows, val, store):
    slots = row.shape[1]
    width = val.shape[1]
    half = rows // 2
    low = jnp.where(row >= half, row - half, row)
    high = key >= half
    both = jnp.concatenate(
        [jnp.where(high, 0.0, val).astype(bf), jnp.where(high, val, 0.0).astype(bf)], axis=1
    )
    size = half // PARTS
    at = lax.broadcasted_iota(jnp.int32, (size, slots), 0).astype(f32)
    for p in range(PARTS):
        hot = jnp.where(at == low - p * size, 1.0, 0.0).astype(bf)
        sums = jnp.dot(hot, both, preferred_element_type=f32)
        store(p * size, sums[:, :width])
        store(half + p * size, sums[:, width:])


def stage_kernel(from_ref, to_ref, sem):
    copy = pltpu.make_async_copy(from_ref, to_ref, sem)
    copy.start()
    copy.wait()


def stage(a):
    return pl.pallas_call(
        stage_kernel,
        out_shape=pltpu.VMEM(a.shape, a.dtype),
        in_specs=[pl.BlockSpec(memory_space=pltpu.HBM)],
        out_specs=pl.BlockSpec(memory_space=pltpu.VMEM),
        scratch_shapes=[pltpu.SemaphoreType.DMA],
        cost_estimate=pl.CostEstimate(flops=0, bytes_accessed=2 * a.size, transcendentals=0),
        compiler_params=pltpu.CompilerParams(vmem_limit_bytes=8 << 20),
        name="stage",
    )(pltpu.with_memory_space_constraint(a, pltpu.HBM))


def rem_kernel(first, count, where_ref, got_ref, slab_ref, r0, r1, r2, r3, sum_ref):
    tables, _, width = slab_ref.shape
    sources, cap = got_ref.shape[0], CAP
    slots = sources * cap
    rem_rows = sum_ref.shape[0]
    keys = unpack_keys(got_ref[:, tables * cap :])
    rows = key_rows(keys, tables)
    sub_rows = r0.shape[2]
    at = where_ref[1]
    along_z = where_ref[0] == 0
    for k in range(count):
        t = first + k
        g = got_ref[:, t * cap : (t + 1) * cap].reshape(slots, width).astype(f32)
        q, m = key_lanes(keys, t)
        val = g * pick(q, slab_ref[t])


        def store(at, sums):
            sum_ref[at : at + sums.shape[0]] = sums.astype(bf)

        spread(rows[tables + t : tables + t + 1], m, rem_rows, val, store)
        for rel, ref in enumerate((r0, r1, r2, r3)):
            far = (at + rel) % 4
            for sub in range(4):
                block = jnp.where(along_z, far * NY + sub, sub * NY + far)
                start = pl.multiple_of(block * sub_rows, sub_rows)
                ref[k, sub] = sum_ref[pl.ds(start, sub_rows), :]


def rem_parts(first, count, where, got, slab, rem_rows):
    sources, _, width = got.shape
    slots = sources * CAP
    sub = rem_rows // (NZ * NY)
    piece = jax.ShapeDtypeStruct((count, 4, sub, width), bf)
    return pl.pallas_call(
        functools.partial(rem_kernel, first, count),
        out_shape=(piece,) * 4,
        grid_spec=pltpu.PrefetchScalarGridSpec(
            num_scalar_prefetch=1,
            grid=(),
            in_specs=[pl.BlockSpec(memory_space=pltpu.VMEM)] * 2,
            out_specs=[pl.BlockSpec(memory_space=pltpu.VMEM)] * 4,
            scratch_shapes=[pltpu.VMEM((rem_rows, width), bf)],
        ),
        cost_estimate=pl.CostEstimate(
            flops=count * 4 * slots * rem_rows * width, bytes_accessed=1 << 22, transcendentals=0
        ),
        compiler_params=pltpu.CompilerParams(vmem_limit_bytes=12 << 20),
        name="rem_parts",
    )(where, got, slab)


def lane_mean(x):
    width = x.shape[1]
    square = x * x
    high = square.astype(bf)
    low = (square - high.astype(f32)).astype(bf)
    ones = jnp.full((width, width), 1.0 / width, bf)
    return jnp.dot(high, ones, preferred_element_type=f32) + jnp.dot(
        low, ones, preferred_element_type=f32
    )


def quot_kernel(first, tables, g_ref, pack_ref, rtab_ref, slab_ref, acc_ref, *refs):
    quot_ref, out_ref, key_ref, row_ref, sum_ref, col_ref, done_ref = refs[-7:]
    sources, cap, width = g_ref.shape
    slots = sources * cap
    quot_rows = quot_ref.shape[1]
    step = pl.program_id(0)
    t = first + step

    @pl.when(step == 0)
    def _():
        keys = unpack_keys(pack_ref[...])
        key_ref[...] = keys
        row_ref[...] = key_rows(keys, tables)
        col_ref[...] = acc_ref[...].T

    g = g_ref[...].reshape(slots, width).astype(f32)
    q, m = key_lanes(key_ref[...], t)
    val = g * pick(m, rtab_ref[0])

    def store(at, sums):
        sum_ref[at : at + sums.shape[0]] = sums

    spread(row_ref[pl.ds(t, 1), :], q, quot_rows, val, store)
    size = quot_rows // 4
    for at in range(0, quot_rows, size):
        part = slice(at, at + size)
        grad = sum_ref[part]
        col = lax.broadcasted_iota(jnp.int32, (size, tables), 1)
        old = jnp.sum(jnp.where(col == t, col_ref[part], 0.0), axis=1, keepdims=True)
        acc = old + lane_mean(grad)
        new = slab_ref[0, part].astype(f32) - step_rate * grad * lax.rsqrt(acc + epsilon)
        quot_ref[0, part] = new.astype(bf)
        lane = lax.broadcasted_iota(jnp.int32, (size, width), 1)
        done_ref[part] = jnp.where(lane == step, acc, done_ref[part])

    @pl.when(step == pl.num_programs(0) - 1)
    def _():
        out_ref[...] = done_ref[...].T[: out_ref.shape[0]]


def quot_update(first, count, got, rtab, slab, accum, old=None):
    sources, _, width = got.shape
    tables, rem_rows, _ = rtab.shape
    quot_rows = slab.shape[1]
    slots = sources * CAP
    rtab = pltpu.with_memory_space_constraint(rtab, pltpu.HBM)
    slab = pltpu.with_memory_space_constraint(slab, pltpu.HBM)
    ins, extra, alias = [got, got, rtab, slab, accum], [], {}
    if old is not None:
        ins.append(old)
        extra = [pl.BlockSpec(memory_space=pltpu.HBM)]
        alias = {len(ins) - 1: 0}
    return pl.pallas_call(
        functools.partial(quot_kernel, first, tables),
        out_shape=(
            pltpu.HBM(slab.shape, bf),
            jax.ShapeDtypeStruct((tables, quot_rows), f32),
        ),
        grid=(count,),
        in_specs=[
            pl.BlockSpec((sources, CAP, width), lambda t: (0, first + t, 0)),
            pl.BlockSpec((sources, KEY_ROWS, width), lambda t: (0, tables * CAP // KEY_ROWS, 0)),
            pl.BlockSpec((1, rem_rows, width), lambda t: (first + t, 0, 0)),
            pl.BlockSpec((1, quot_rows, width), lambda t: (first + t, 0, 0)),
            pl.BlockSpec((tables, quot_rows), lambda t: (0, 0)),
        ]
        + extra,
        out_specs=(
            pl.BlockSpec((1, quot_rows, width), lambda t: (first + t, 0, 0)),
            pl.BlockSpec((tables, quot_rows), lambda t: (0, 0)),
        ),
        scratch_shapes=[
            pltpu.VMEM((slots, width), bf),
            pltpu.VMEM((width, slots), f32),
            pltpu.VMEM((quot_rows, width), f32),
            pltpu.VMEM((quot_rows, tables), f32),
            pltpu.VMEM((quot_rows, width), f32),
        ],
        input_output_aliases=alias,
        cost_estimate=pl.CostEstimate(
            flops=count * 4 * slots * rem_rows * width, bytes_accessed=1 << 23, transcendentals=0
        ),
        compiler_params=pltpu.CompilerParams(vmem_limit_bytes=14 << 20),
        name="quot_update",
    )(*ins)


def turn(a, s, flip):
    return lax.ppermute(a, CZY, turn_pairs(s, flip))


def add(*parts):
    total = parts[0].astype(f32)
    for p in parts[1:]:
        total = total + p.astype(f32)
    return total


def ring_scatter(low, high, flip):
    far_low = turn(low[2], 1, flip)
    near_low = turn(low[3], -1, flip)
    far_high = turn(high[2], -1, flip)
    near_high = turn(high[1], 1, flip)
    sum_low = turn(add(low[1], far_low).astype(bf), 1, flip)
    sum_high = turn(add(high[3], far_high).astype(bf), -1, flip)
    return add(low[0], near_low, sum_low), add(high[0], near_high, sum_high)


def ring_gather(low, high, flip):
    prev_low = turn(low, 1, flip)
    next_high = turn(high, -1, flip)
    next_low = turn(low, -1, flip)
    prev_high = turn(high, 1, flip)
    far_low = turn(prev_low, 1, flip)
    far_high = turn(next_high, -1, flip)
    return [low, next_low, far_low, prev_low], [high, next_high, far_high, prev_high]


def place_kernel(rels, where_ref, *refs):
    count = 2 * len(rels)
    ins = refs[:count]
    out_ref, buf, in_sem, out_sem = refs[-4:]
    half = out_ref.shape[0] // 2
    at = where_ref[1]

    def move(along_z):
        takes = [pltpu.make_async_copy(ins[i], buf.at[i], in_sem.at[i]) for i in range(count)]
        puts = []
        for i in range(count):
            far = (at + rels[i // 2]) % 4
            tabs = pl.ds(i % 2 * half, half)
            to = out_ref.at[tabs, far] if along_z else out_ref.at[tabs, :, far]
            puts.append(pltpu.make_async_copy(buf.at[i], to, out_sem.at[i]))
        for take in takes:
            take.start()
        for take, put in zip(takes, puts):
            take.wait()
            put.start()
        for put in puts:
            put.wait()

    pl.when(where_ref[0] == 0)(lambda: move(True))
    pl.when(where_ref[0] != 0)(lambda: move(False))


def place(rels, where, pieces, shape, old=None):
    ins = [x for lh in pieces for x in lh]
    count = len(ins)
    alias = {}
    if old is not None:
        ins.append(old)
        alias = {len(ins): 0}
    hbm = pl.BlockSpec(memory_space=pl.ANY)
    return pl.pallas_call(
        functools.partial(place_kernel, rels),
        out_shape=jax.ShapeDtypeStruct(shape, bf),
        grid_spec=pltpu.PrefetchScalarGridSpec(
            num_scalar_prefetch=1,
            grid=(),
            in_specs=[hbm] * len(ins),
            out_specs=hbm,
            scratch_shapes=[
                pltpu.VMEM((count,) + ins[0].shape, bf),
                pltpu.SemaphoreType.DMA((count,)),
                pltpu.SemaphoreType.DMA((count,)),
            ],
        ),
        input_output_aliases=alias,
        cost_estimate=pl.CostEstimate(flops=0, bytes_accessed=len(rels) << 21, transcendentals=0),
        compiler_params=pltpu.CompilerParams(vmem_limit_bytes=8 << 20),
        name="place",
    )(where, *ins)


def rank_sums(feat, cot, cross_in, cross_out, ready):
    where = jnp.stack([lax.axis_index("c"), lax.axis_index("x")]).astype(jnp.int32)
    swap = lambda a: lax.ppermute(a, "c", [(0, 1), (1, 0)])
    both = rank_parts(where, feat, cot, cross_in, cross_out)
    parts = [None] * NX
    for k in (2, 1, 3, 0):
        parts[k] = add(both[NX + k], swap(both[k])).astype(bf)
    far = lax.ppermute(parts[2], "x", ring(NX, 2))
    nxt = lax.ppermute(parts[1], "x", ring(NX, 1))
    prev = lax.ppermute(parts[3], "x", ring(NX, 3))
    mine = add(parts[0], far, nxt, prev).astype(bf)
    mine, ready = lax.optimization_barrier((mine, ready))
    far = lax.ppermute(mine, "x", ring(NX, 2))
    prev = lax.ppermute(mine, "x", ring(NX, 1))
    nxt = lax.ppermute(mine, "x", ring(NX, 3))
    own = (mine, prev, far, nxt)
    return own + tuple(swap(a) for a in own), ready


def update_kernel(own_ref, next_ref, far_ref, prev_ref, acc_ref, tab_ref, new_ref, out_ref):
    tables, subs, rows, width = own_ref.shape
    accs = acc_ref[...].T
    lane = lax.broadcasted_iota(jnp.int32, (rows, width), 1)
    done = jnp.zeros((rows, width), f32)
    for i in range(tables * subs):
        t, s = divmod(i, subs)
        grad = (own_ref[t, s].astype(f32) + far_ref[t, s].astype(f32)) + (
            next_ref[t, s].astype(f32) + prev_ref[t, s].astype(f32)
        )
        acc = accs[:, i : i + 1] + lane_mean(grad)
        new = tab_ref[t, s].astype(f32) - step_rate * grad * lax.rsqrt(acc + epsilon)
        new_ref[t, s] = new.astype(bf)
        done = jnp.where(lane == i, acc, done)
    out_ref[...] = done.T[: tables * subs]


def update(ring_parts, acc, tab):
    vmem = pl.BlockSpec(memory_space=pltpu.VMEM)
    tables, subs, rows, _ = tab.shape
    new, out = pl.pallas_call(
        update_kernel,
        out_shape=(
            jax.ShapeDtypeStruct(tab.shape, bf),
            jax.ShapeDtypeStruct((tables * subs, rows), f32),
        ),
        in_specs=[vmem] * 6,
        out_specs=(vmem, vmem),
        cost_estimate=pl.CostEstimate(flops=tab.size * 8, bytes_accessed=4 << 20, transcendentals=0),
        compiler_params=pltpu.CompilerParams(vmem_limit_bytes=12 << 20),
        name="update",
    )(*ring_parts, acc.reshape(tables * subs, rows), tab)
    return out.reshape(acc.shape), new


def device_step(
    features, cotangent, cross_in, cross_out, bias, dest_shard, quot_row, rem_row,
    quot_slab, quot_accum, rem_table, rem_accum,
):
    samples = features.shape[0]
    tables = quot_slab.shape[0]
    width = quot_slab.shape[2]
    rem_rows = rem_table.shape[1]
    rows = NZ * NY
    cap = CAP
    ci, zi, yi = lax.axis_index("c"), lax.axis_index("z"), lax.axis_index("y")

    target = dest_shard[:, :, 0]
    onehot = target[:, :, None] == jnp.arange(rows, dtype=jnp.int32)[None, None, :]
    lower = (
        jnp.arange(samples, dtype=jnp.int32)[:, None]
        >= jnp.arange(samples, dtype=jnp.int32)[None, :]
    ).astype(bf)
    running = jnp.einsum("ij,tjn->tin", lower, onehot.astype(bf), preferred_element_type=f32)
    slot_index = jnp.sum(jnp.where(onehot, running, 0.0), axis=2).astype(jnp.int32) - 1
    position = target * cap + slot_index
    digits = digit_lanes(quot_row, rem_row, width)

    position = position.reshape(tables, 1, samples)
    pieces, (position, digits) = rank_sums(
        features, cotangent, cross_in, cross_out, (position, digits)
    )
    xi = lax.axis_index("x")
    send = pooled_dispatch(
        jnp.stack([ci, xi]).astype(jnp.int32), pieces, cotangent, cross_out, cross_in,
        bias.reshape(1, -1), position, digits, rows, cap, width,
    )
    got = lax.all_to_all(send, ("z", "y"), split_axis=0, concat_axis=0, tiled=True)
    slab = stage(quot_slab)
    along_z = ci == 0
    at_one = jnp.where(along_z, zi, yi)
    at_two = jnp.where(along_z, yi, zi)
    where = jnp.stack([ci, at_one, at_one]).astype(jnp.int32)
    half = tables // 2
    low = rem_parts(0, half, where, got, slab, rem_rows)
    high = rem_parts(half, half, where, got, slab, rem_rows)

    one_low, one_high = ring_scatter(low, high, False)
    ring_low, ring_high = ring_gather(one_low.astype(bf), one_high.astype(bf), True)
    share = rem_rows // rows
    view = (tables, NZ, NY, share)

    def quarter(a):
        a = a.reshape(view + a.shape[2:])
        return jnp.where(
            along_z,
            lax.dynamic_index_in_dim(a, zi, 1, keepdims=False),
            lax.dynamic_index_in_dim(a, yi, 2, keepdims=False),
        )

    acc_in, tab_in = quarter(rem_accum), quarter(rem_table)
    acc_low, new_low = update(ring_low, acc_in[:half], tab_in[:half])
    acc_high, new_high = update(ring_high, acc_in[half:], tab_in[half:])
    acc = jnp.concatenate([acc_low, acc_high], axis=0)
    rem_acc_out = lax.dynamic_index_in_dim(acc, at_two, 1, keepdims=False)
    all_low, all_high = ring_gather(new_low, new_high, False)
    shape = (tables, NZ, NY, share, width)
    near = [(all_low[k], all_high[k]) for k in (0, 1, 3)]
    rem_out = place((0, 1, 3), where, near, shape)
    rem_out = place((2,), where, [(all_low[2], all_high[2])], shape, rem_out)
    rem_out = rem_out.reshape(tables, rem_rows, width)

    quot_out, acc_low = quot_update(0, half, got, rem_table, quot_slab, quot_accum)
    quot_out, acc_high = quot_update(half, half, got, rem_table, quot_slab, quot_accum, quot_out)
    quot_acc_out = jnp.concatenate([acc_low[:half], acc_high[:half]], axis=0)
    return (quot_out, quot_acc_out, rem_out, rem_acc_out)


def solution(mesh):
    fine = Mesh(mesh.devices.reshape(NX, NC, NZ, NY), ("x", "c", "z", "y"))
    T, R = ("x", "c"), ("z", "y")
    return jax.shard_map(
        device_step,
        mesh=fine,
        in_specs=(
            P(R, T), P(R, T), P(T, None), P(T, None), P(T), P(T, R, None), P(T, R), P(T, R),
            P(T, R, None), P(T, R), P(T, None, None), P(T, None),
        ),
        out_specs=(P(T, R, None), P(T, R), P(T, None, None), P(T, R)),
        check_vma=False,
    )
```

```python
import functools

import jax
import jax.numpy as jnp
from jax import lax
from jax.experimental import pallas as pl
from jax.experimental.pallas import tpu as pltpu
from jax.sharding import Mesh
from jax.sharding import PartitionSpec as P


step_rate = 0.3
epsilon = 1e-06
bf = jnp.bfloat16
f32 = jnp.float32
NX, NC, NZ, NY = 4, 2, 4, 4
CZY = ("c", "z", "y")
NT = (((1,), (1,)), ((), ()))


def ring(n, s):
    return [(i, (i + s) % n) for i in range(n)]


def spot(c, z, y):
    return (c * NZ + z) * NY + y


def turn_pairs(s, flip):
    out = []
    for c in range(NC):
        for z in range(NZ):
            for y in range(NY):
                if (c == 0) != flip:
                    to = spot(c, (z + s) % NZ, y)
                else:
                    to = spot(c, z, (y + s) % NY)
                out.append((spot(c, z, y), to))
    return out


def rank_kernel(at_ref, feat_ref, cot_ref, ci_ref, co_ref, *refs):
    outs, (feat_buf, cot_buf, ci_buf, co_buf, acc_ref, sem) = refs[: 2 * NX], refs[2 * NX :]
    chunks, samples, tile = feat_buf.shape
    rank = ci_ref.shape[1]

    def loads(k):
        at = pl.ds(k * tile, tile)
        return (
            pltpu.make_async_copy(feat_ref.at[:, at], feat_buf.at[k], sem.at[0, k]),
            pltpu.make_async_copy(ci_ref.at[at], ci_buf.at[k], sem.at[1, k]),
            pltpu.make_async_copy(cot_ref.at[:, at], cot_buf.at[k], sem.at[2, k]),
            pltpu.make_async_copy(co_ref.at[at], co_buf.at[k], sem.at[3, k]),
        )

    copies = [loads(k) for k in range(chunks)]
    for four in copies:
        for copy in four:
            copy.start()
    for k in range(chunks):
        for copy in copies[k]:
            copy.wait()
        feat = feat_buf[k]
        product = (cot_buf[k].astype(f32) * feat.astype(f32)).astype(bf)
        left = jnp.dot(feat, ci_buf[k], preferred_element_type=f32)
        right = jnp.dot(product, co_buf[k], preferred_element_type=f32)
        if k:
            acc_ref[:, :rank] += left
            acc_ref[:, rank:] += right
        else:
            acc_ref[:, :rank] = left
            acc_ref[:, rank:] = right
    size = samples // (NC * NX)
    for i, out in enumerate(outs):
        c = at_ref[0] if i >= NX else 1 - at_ref[0]
        row = (c * NX + (at_ref[1] + i % NX) % NX) * size
        out[...] = acc_ref[pl.ds(pl.multiple_of(row, size), size), :].astype(out.dtype)


def rank_parts(where, feat, cot, cross_in, cross_out):
    samples, depth = feat.shape
    rank = cross_in.shape[1]
    chunks = 2
    tile = depth // chunks
    ins = [
        pltpu.with_memory_space_constraint(a, pltpu.HBM)
        for a in (feat, cot, cross_in, cross_out)
    ]
    shape = (samples // (NC * NX), 2 * rank)
    return pl.pallas_call(
        rank_kernel,
        out_shape=(jax.ShapeDtypeStruct(shape, bf),) * NX
        + (jax.ShapeDtypeStruct(shape, f32),) * NX,
        grid_spec=pltpu.PrefetchScalarGridSpec(
            num_scalar_prefetch=1,
            grid=(),
            in_specs=[pl.BlockSpec(memory_space=pltpu.HBM)] * 4,
            out_specs=[pl.BlockSpec(memory_space=pltpu.VMEM)] * (2 * NX),
            scratch_shapes=[
                pltpu.VMEM((chunks, samples, tile), bf),
                pltpu.VMEM((chunks, samples, tile), bf),
                pltpu.VMEM((chunks, tile, rank), bf),
                pltpu.VMEM((chunks, tile, rank), bf),
                pltpu.VMEM((samples, 2 * rank), f32),
                pltpu.SemaphoreType.DMA((4, chunks)),
            ],
        ),
        cost_estimate=pl.CostEstimate(
            flops=4 * samples * depth * rank, bytes_accessed=8 << 20, transcendentals=0
        ),
        compiler_params=pltpu.CompilerParams(vmem_limit_bytes=16 << 20),
        name="rank_parts",
    )(where, *ins)


def join_kernel(at_ref, *refs):
    pieces, rank_ref = refs[:-1], refs[-1]
    size = pieces[0].shape[0]
    for i, piece in enumerate(pieces):
        c = at_ref[0] if i < NX else 1 - at_ref[0]
        row = (c * NX + (at_ref[1] + NX - i % NX) % NX) * size
        rank_ref[pl.ds(pl.multiple_of(row, size), size), :] = piece[...]


def join(where, pieces):
    size, width = pieces[0].shape
    vmem = pl.BlockSpec(memory_space=pltpu.VMEM)
    return pl.pallas_call(
        join_kernel,
        out_shape=pltpu.VMEM((len(pieces) * size, width), bf),
        grid_spec=pltpu.PrefetchScalarGridSpec(
            num_scalar_prefetch=1, grid=(), in_specs=[vmem] * len(pieces), out_specs=vmem
        ),
        compiler_params=pltpu.CompilerParams(vmem_limit_bytes=8 << 20),
        name="join",
    )(where, *pieces)


def pooled_kernel(first, rank_ref, *refs):
    cot_ref, co_ref, ci_ref, bias_ref, pos_ref, dig_ref = refs[:6]
    outs, (key_ref,) = refs[6:10], refs[10:]
    rank = co_ref.shape[1]
    width, cap = key_ref.shape[1], CAP

    dests = 4 * outs[0].shape[0]
    half = (outs[0].shape[1] - KEY_ROWS) // cap
    samples = cot_ref.shape[0]
    here = pos_ref.shape[0]
    step = pl.program_id(0)
    gate = (
        lax.dot_general(rank_ref[:, :rank], co_ref[...], NT, preferred_element_type=f32)
        + bias_ref[...]
    )
    back = lax.dot_general(rank_ref[:, rank:], ci_ref[...], NT, preferred_element_type=f32)
    pooled = (cot_ref[...].astype(f32) * (gate + 1.0) + back).astype(bf)
    slot = lax.broadcasted_iota(jnp.int32, (dests * cap, samples), 0)
    owner = lax.broadcasted_iota(jnp.int32, (samples, width), 1) % LANES // DIGITS
    keys = jnp.zeros((dests * cap, width), f32)
    for k in range(here):
        t = step * here + k
        placed = jnp.where(slot == pos_ref[k], 1.0, 0.0).astype(bf)
        digits = jnp.where(owner == first + t, dig_ref[...].astype(f32), 0.0).astype(bf)
        both = jnp.concatenate([pooled[:, k * width : (k + 1) * width], digits], axis=1)
        rows = jnp.dot(placed, both, preferred_element_type=f32)
        spot = pl.ds(pl.multiple_of(t * cap, KEY_ROWS), cap)
        vals = rows[:, :width].astype(bf).reshape(4, dests // 4, cap, width)
        for r, out in enumerate(outs):
            out[:, spot] = vals[r]
        keys = keys + rows[:, width:]

    @pl.when(step == 0)
    def _():
        key_ref[...] = keys

    @pl.when(step > 0)
    def _():
        key_ref[...] += keys

    @pl.when(step == pl.num_programs(0) - 1)
    def _():
        parts = key_ref[...].reshape(dests, cap // KEY_ROWS, KEY_ROWS, width)
        group = lax.broadcasted_iota(jnp.int32, (dests, KEY_ROWS, width), 2) // LANES
        packed = jnp.zeros((dests, KEY_ROWS, width), f32)
        for k in range(cap // KEY_ROWS):
            packed = jnp.where(group == k, parts[:, k], packed)
        for r, out in enumerate(outs):
            out[:, half * cap :] = packed[r * (dests // 4) : (r + 1) * (dests // 4)].astype(bf)


def pooled_dispatch(first, count, rank, cot, co, ci, bias, pos, digits, dests, cap, width):
    samples = cot.shape[0]
    pair = 2
    skip = first // pair
    out = jax.ShapeDtypeStruct((dests // 4, count * cap + KEY_ROWS, width), bf)
    return pl.pallas_call(
        functools.partial(pooled_kernel, first),
        out_shape=(out,) * 4,
        grid=(count // pair,),
        in_specs=[
            pl.BlockSpec(memory_space=pltpu.VMEM),
            pl.BlockSpec((samples, pair * width), lambda i: (0, skip + i)),
            pl.BlockSpec((pair * width, co.shape[1]), lambda i: (skip + i, 0)),
            pl.BlockSpec((pair * width, co.shape[1]), lambda i: (skip + i, 0)),
            pl.BlockSpec((1, pair * width), lambda i: (0, skip + i)),
            pl.BlockSpec((pair, 1, samples), lambda i: (skip + i, 0, 0)),
            pl.BlockSpec(digits.shape, lambda i: (0, 0)),
        ],
        out_specs=[pl.BlockSpec(out.shape, lambda i: (0, 0, 0))] * 4,
        scratch_shapes=[pltpu.VMEM((dests * cap, width), f32)],
        cost_estimate=pl.CostEstimate(
            flops=count * samples * width * 4 * (co.shape[1] + dests * cap),
            bytes_accessed=4 << 20,
            transcendentals=0,
        ),
        compiler_params=pltpu.CompilerParams(vmem_limit_bytes=12 << 20),
        name="pooled_dispatch",
    )(rank, cot, co, ci, bias, pos, digits)


DIGITS, QB, MB, LANES, KEY_ROWS, CAP = 4, 32, 64, 32, 16, 48
PARTS = 2


def digit_lanes(q, m, width):
    parts = jnp.stack([q // QB, q % QB, m // MB, m % MB], axis=1)
    parts = parts.reshape(-1, q.shape[1])
    parts = jnp.concatenate([parts] * (CAP // KEY_ROWS), axis=0)
    parts = jnp.pad(parts, ((0, width - parts.shape[0]), (0, 0)))
    return parts.T.astype(bf)


def unpack_keys(packed):
    sources, _, width = packed.shape
    group = lax.broadcasted_iota(jnp.int32, packed.shape, 2) // LANES
    packed = packed.astype(f32)
    parts = [jnp.where(group == k, packed, 0.0)[:, None] for k in range(CAP // KEY_ROWS)]
    return jnp.concatenate(parts, axis=1).reshape(sources * CAP, width).astype(bf)


def key_rows(keys, tables):
    width = keys.shape[1]
    lane = lax.broadcasted_iota(jnp.int32, (width, width), 0) % LANES
    col = lax.broadcasted_iota(jnp.int32, (width, width), 1)
    t = col % tables
    base = DIGITS * t + jnp.where(col >= tables, 2, 0)
    high = jnp.where(col >= tables, MB, QB).astype(f32)
    comb = jnp.where(lane == base, high, jnp.where(lane == base + 1, 1.0, 0.0))
    comb = jnp.where(col < 2 * tables, comb, 0.0).astype(bf)
    return jnp.dot(keys, comb, preferred_element_type=f32).T


def key_lanes(keys, t):
    width = keys.shape[1]
    lane = lax.broadcasted_iota(jnp.int32, (width, 2 * width), 0) % LANES - DIGITS * t
    side = lax.broadcasted_iota(jnp.int32, (width, 2 * width), 1) >= width
    lane = jnp.where(side, lane - 2, lane)
    high = jnp.where(side, float(MB), float(QB))
    comb = jnp.where(lane == 0, high, jnp.where(lane == 1, 1.0, 0.0)).astype(bf)
    out = jnp.dot(keys, comb, preferred_element_type=f32)
    return out[:, :width], out[:, width:]


def pick(key, tab):
    slots, width = key.shape
    half = tab.shape[0] // 2
    both = jnp.concatenate([tab[:half], tab[half:]], axis=1)
    size = slots // PARTS
    out = []
    for p in range(PARTS):
        part = key[p * size : (p + 1) * size]
        high = part >= half
        low = jnp.where(high, part - half, part)
        lane = lax.broadcasted_iota(jnp.int32, (size, width), 1).astype(f32)
        hot = jnp.concatenate(
            [jnp.where(low - j == lane, 1.0, 0.0).astype(bf) for j in range(0, half, width)],
            axis=1,
        )
        got = jnp.dot(hot, both, preferred_element_type=f32)
        out.append(jnp.where(high, got[:, width:], got[:, :width]))
    return jnp.concatenate(out, axis=0)


def spread(row, key, rows, val, store):
    slots = row.shape[1]
    width = val.shape[1]
    half = rows // 2
    low = jnp.where(row >= half, row - half, row)
    high = key >= half
    both = jnp.concatenate(
        [jnp.where(high, 0.0, val).astype(bf), jnp.where(high, val, 0.0).astype(bf)], axis=1
    )
    size = half // PARTS
    at = lax.broadcasted_iota(jnp.int32, (size, slots), 0).astype(f32)
    for p in range(PARTS):
        hot = jnp.where(at == low - p * size, 1.0, 0.0).astype(bf)
        sums = jnp.dot(hot, both, preferred_element_type=f32)
        store(p * size, sums[:, :width])
        store(half + p * size, sums[:, width:])


def stage_kernel(*refs):
    sem = refs[-1]
    count = len(refs) // 2
    copies = [pltpu.make_async_copy(refs[i], refs[count + i], sem.at[i]) for i in range(count)]
    for copy in copies:
        copy.start()
    for copy in copies:
        copy.wait()


def stage(*arrays):
    size = sum(a.size for a in arrays)
    return pl.pallas_call(
        stage_kernel,
        out_shape=[pltpu.VMEM(a.shape, a.dtype) for a in arrays],
        in_specs=[pl.BlockSpec(memory_space=pltpu.HBM)] * len(arrays),
        out_specs=[pl.BlockSpec(memory_space=pltpu.VMEM)] * len(arrays),
        scratch_shapes=[pltpu.SemaphoreType.DMA((len(arrays),))],
        cost_estimate=pl.CostEstimate(flops=0, bytes_accessed=4 * size, transcendentals=0),
        compiler_params=pltpu.CompilerParams(vmem_limit_bytes=8 << 20),
        name="stage",
    )(*[pltpu.with_memory_space_constraint(a, pltpu.HBM) for a in arrays])


def all_keys(refs, at=None):
    keys = [ref[...] if at is None else ref[:, at:] for ref in refs]
    return unpack_keys(jnp.concatenate(keys, axis=0))


def all_rows(refs, at, cap):
    rows = [ref[:, at : at + cap] for ref in refs]
    rows = [row.reshape(-1, row.shape[-1]) for row in rows]
    return jnp.concatenate(rows, axis=0).astype(f32)


def rem_kernel(first, count, where_ref, *refs):
    (slab_ref, r0, r1, r2, r3, sum_ref), parts = refs[-6:], refs[:-6]
    tables, _, _ = slab_ref.shape
    cap = CAP
    rem_rows = sum_ref.shape[0]
    keys = all_keys(parts, count * cap)
    rows = key_rows(keys, tables)
    sub_rows = r0.shape[2]
    at = where_ref[1]
    along_z = where_ref[0] == 0
    for k in range(count):
        t = first + k
        g = all_rows(parts[:4], k * cap, cap)
        q, m = key_lanes(keys, t)
        val = g * pick(q, slab_ref[t])


        def store(at, sums):
            sum_ref[at : at + sums.shape[0]] = sums.astype(bf)

        spread(rows[tables + t : tables + t + 1], m, rem_rows, val, store)
        for rel, ref in enumerate((r0, r1, r2, r3)):
            far = (at + rel) % 4
            for sub in range(4):
                block = jnp.where(along_z, far * NY + sub, sub * NY + far)
                start = pl.multiple_of(block * sub_rows, sub_rows)
                ref[k, sub] = sum_ref[pl.ds(start, sub_rows), :]


def rem_parts(first, count, where, got, slab, rem_rows):
    _, _, width = slab.shape
    slots = NZ * NY * CAP
    ins = got
    sub = rem_rows // (NZ * NY)
    piece = jax.ShapeDtypeStruct((count, 4, sub, width), bf)
    return pl.pallas_call(
        functools.partial(rem_kernel, first, count),
        out_shape=(piece,) * 4,
        grid_spec=pltpu.PrefetchScalarGridSpec(
            num_scalar_prefetch=1,
            grid=(),
            in_specs=[pl.BlockSpec(memory_space=pltpu.VMEM)] * (len(ins) + 1),
            out_specs=[pl.BlockSpec(memory_space=pltpu.VMEM)] * 4,
            scratch_shapes=[pltpu.VMEM((rem_rows, width), bf)],
        ),
        cost_estimate=pl.CostEstimate(
            flops=count * 4 * slots * rem_rows * width, bytes_accessed=1 << 22, transcendentals=0
        ),
        compiler_params=pltpu.CompilerParams(vmem_limit_bytes=12 << 20),
        name="rem_parts",
    )(where, *ins, slab)


def lane_mean(x):
    width = x.shape[1]
    square = x * x
    high = square.astype(bf)
    low = (square - high.astype(f32)).astype(bf)
    ones = jnp.full((width, width), 1.0 / width, bf)
    return jnp.dot(high, ones, preferred_element_type=f32) + jnp.dot(
        low, ones, preferred_element_type=f32
    )


def quot_kernel(first, tables, *refs):
    parts, packs, (rtab_ref, slab_ref, acc_ref), refs = refs[:4], refs[4:8], refs[8:11], refs[11:]
    quot_ref, out_ref, key_ref, row_ref, sum_ref, col_ref, done_ref = refs[-7:]
    cap, width = parts[0].shape[1:]
    quot_rows = quot_ref.shape[1]
    step = pl.program_id(0)
    t = first + step

    @pl.when(step == 0)
    def _():
        keys = all_keys(packs)
        key_ref[...] = keys
        row_ref[...] = key_rows(keys, tables)
        col_ref[...] = acc_ref[...].T

    g = all_rows(parts, 0, cap)
    q, m = key_lanes(key_ref[...], t)
    val = g * pick(m, rtab_ref[0])

    def store(at, sums):
        sum_ref[at : at + sums.shape[0]] = sums

    spread(row_ref[pl.ds(t, 1), :], q, quot_rows, val, store)
    size = quot_rows // 4
    for at in range(0, quot_rows, size):
        part = slice(at, at + size)
        grad = sum_ref[part]
        col = lax.broadcasted_iota(jnp.int32, (size, tables), 1)
        old = jnp.sum(jnp.where(col == t, col_ref[part], 0.0), axis=1, keepdims=True)
        acc = old + lane_mean(grad)
        new = slab_ref[0, part].astype(f32) - step_rate * grad * lax.rsqrt(acc + epsilon)
        quot_ref[0, part] = new.astype(bf)
        lane = lax.broadcasted_iota(jnp.int32, (size, width), 1)
        done_ref[part] = jnp.where(lane == step, acc, done_ref[part])

    @pl.when(step == pl.num_programs(0) - 1)
    def _():
        out_ref[...] = done_ref[...].T[: out_ref.shape[0]]


def quot_update(first, count, got, rtab, slab, accum, old=None):
    tables, rem_rows, width = rtab.shape
    quot_rows = slab.shape[1]
    slots = NZ * NY * CAP
    rtab = pltpu.with_memory_space_constraint(rtab, pltpu.HBM)
    slab = pltpu.with_memory_space_constraint(slab, pltpu.HBM)
    ins, extra, alias = [*got, *got, rtab, slab, accum], [], {}
    if old is not None:
        ins.append(old)
        extra = [pl.BlockSpec(memory_space=pltpu.HBM)]
        alias = {len(ins) - 1: 0}
    return pl.pallas_call(
        functools.partial(quot_kernel, first, tables),
        out_shape=(
            pltpu.HBM(slab.shape, bf),
            jax.ShapeDtypeStruct((tables, quot_rows), f32),
        ),
        grid=(count,),
        in_specs=[
            *[pl.BlockSpec((4, CAP, width), lambda t: (0, t, 0))] * 4,
            *[pl.BlockSpec((4, KEY_ROWS, width), lambda t: (0, count * CAP // KEY_ROWS, 0))]
            * 4,
            pl.BlockSpec((1, rem_rows, width), lambda t: (first + t, 0, 0)),
            pl.BlockSpec((1, quot_rows, width), lambda t: (first + t, 0, 0)),
            pl.BlockSpec((tables, quot_rows), lambda t: (0, 0)),
        ]
        + extra,
        out_specs=(
            pl.BlockSpec((1, quot_rows, width), lambda t: (first + t, 0, 0)),
            pl.BlockSpec((tables, quot_rows), lambda t: (0, 0)),
        ),
        scratch_shapes=[
            pltpu.VMEM((slots, width), bf),
            pltpu.VMEM((width, slots), f32),
            pltpu.VMEM((quot_rows, width), f32),
            pltpu.VMEM((quot_rows, tables), f32),
            pltpu.VMEM((quot_rows, width), f32),
        ],
        input_output_aliases=alias,
        cost_estimate=pl.CostEstimate(
            flops=count * 4 * slots * rem_rows * width, bytes_accessed=1 << 23, transcendentals=0
        ),
        compiler_params=pltpu.CompilerParams(vmem_limit_bytes=14 << 20),
        name="quot_update",
    )(*ins)


def turn(a, s, flip):
    return lax.ppermute(a, CZY, turn_pairs(s, flip))


def add(*parts):
    total = parts[0].astype(f32)
    for p in parts[1:]:
        total = total + p.astype(f32)
    return total


def swap_rows(low, high):
    def first(parts):
        far = turn(parts[2], 2, False)
        return (parts[0], turn(parts[1], 1, False), far, turn(parts[3], 3, False))

    def second(parts):
        parts = [jnp.stack([part[j] for part in parts]) for j in range(4)]
        far = turn(parts[2], 2, True)
        return (parts[0], turn(parts[1], 1, True), far, turn(parts[3], 3, True))

    low, high = first(low), first(high)
    return second(low), second(high)


def ring_scatter(low, high, flip):
    far_low = turn(low[2], 1, flip)
    near_low = turn(low[3], -1, flip)
    far_high = turn(high[2], -1, flip)
    near_high = turn(high[1], 1, flip)
    sum_low = turn(add(low[1], far_low).astype(bf), 1, flip)
    sum_high = turn(add(high[3], far_high).astype(bf), -1, flip)
    return add(low[0], near_low, sum_low), add(high[0], near_high, sum_high)


def ring_gather(low, high, flip):
    prev_low = turn(low, 1, flip)
    next_high = turn(high, -1, flip)
    next_low = turn(low, -1, flip)
    prev_high = turn(high, 1, flip)
    far_low = turn(prev_low, 1, flip)
    far_high = turn(next_high, -1, flip)
    return [low, next_low, far_low, prev_low], [high, next_high, far_high, prev_high]


def place_kernel(rels, where_ref, *refs):
    count = 2 * len(rels)
    ins = refs[:count]
    out_ref, buf, in_sem, out_sem = refs[-4:]
    half = out_ref.shape[0] // 2
    at = where_ref[1]

    def move(along_z):
        takes = [pltpu.make_async_copy(ins[i], buf.at[i], in_sem.at[i]) for i in range(count)]
        puts = []
        for i in range(count):
            far = (at + rels[i // 2]) % 4
            tabs = pl.ds(i % 2 * half, half)
            to = out_ref.at[tabs, far] if along_z else out_ref.at[tabs, :, far]
            puts.append(pltpu.make_async_copy(buf.at[i], to, out_sem.at[i]))
        for take in takes:
            take.start()
        for take, put in zip(takes, puts):
            take.wait()
            put.start()
        for put in puts:
            put.wait()

    pl.when(where_ref[0] == 0)(lambda: move(True))
    pl.when(where_ref[0] != 0)(lambda: move(False))


def place(rels, where, pieces, shape, old=None):
    ins = [x for lh in pieces for x in lh]
    count = len(ins)
    alias = {}
    if old is not None:
        ins.append(old)
        alias = {len(ins): 0}
    hbm = pl.BlockSpec(memory_space=pl.ANY)
    return pl.pallas_call(
        functools.partial(place_kernel, rels),
        out_shape=jax.ShapeDtypeStruct(shape, bf),
        grid_spec=pltpu.PrefetchScalarGridSpec(
            num_scalar_prefetch=1,
            grid=(),
            in_specs=[hbm] * len(ins),
            out_specs=hbm,
            scratch_shapes=[
                pltpu.VMEM((count,) + ins[0].shape, bf),
                pltpu.SemaphoreType.DMA((count,)),
                pltpu.SemaphoreType.DMA((count,)),
            ],
        ),
        input_output_aliases=alias,
        cost_estimate=pl.CostEstimate(flops=0, bytes_accessed=len(rels) << 21, transcendentals=0),
        compiler_params=pltpu.CompilerParams(vmem_limit_bytes=8 << 20),
        name="place",
    )(where, *ins)


def rank_sums(feat, cot, cross_in, cross_out, ready):
    where = jnp.stack([lax.axis_index("c"), lax.axis_index("x")]).astype(jnp.int32)
    swap = lambda a: lax.ppermute(a, "c", [(0, 1), (1, 0)])
    both = rank_parts(where, feat, cot, cross_in, cross_out)
    parts = [None] * NX
    for k in (2, 1, 3, 0):
        parts[k] = add(both[NX + k], swap(both[k])).astype(bf)
    far = lax.ppermute(parts[2], "x", ring(NX, 2))
    nxt = lax.ppermute(parts[1], "x", ring(NX, 1))
    prev = lax.ppermute(parts[3], "x", ring(NX, 3))
    mine = add(parts[0], far, nxt, prev).astype(bf)
    mine, ready = lax.optimization_barrier((mine, ready))
    far = lax.ppermute(mine, "x", ring(NX, 2))
    prev = lax.ppermute(mine, "x", ring(NX, 1))
    nxt = lax.ppermute(mine, "x", ring(NX, 3))
    own = (mine, prev, far, nxt)
    return own + tuple(swap(a) for a in own), ready


def update_kernel(own_ref, next_ref, far_ref, prev_ref, acc_ref, tab_ref, new_ref, out_ref):
    tables, subs, rows, width = own_ref.shape
    accs = acc_ref[...].T
    lane = lax.broadcasted_iota(jnp.int32, (rows, width), 1)
    done = jnp.zeros((rows, width), f32)
    for i in range(tables * subs):
        t, s = divmod(i, subs)
        grad = (own_ref[t, s].astype(f32) + far_ref[t, s].astype(f32)) + (
            next_ref[t, s].astype(f32) + prev_ref[t, s].astype(f32)
        )
        acc = accs[:, i : i + 1] + lane_mean(grad)
        new = tab_ref[t, s].astype(f32) - step_rate * grad * lax.rsqrt(acc + epsilon)
        new_ref[t, s] = new.astype(bf)
        done = jnp.where(lane == i, acc, done)
    out_ref[...] = done.T[: tables * subs]


def update(ring_parts, acc, tab):
    vmem = pl.BlockSpec(memory_space=pltpu.VMEM)
    tables, subs, rows, _ = tab.shape
    new, out = pl.pallas_call(
        update_kernel,
        out_shape=(
            jax.ShapeDtypeStruct(tab.shape, bf),
            jax.ShapeDtypeStruct((tables * subs, rows), f32),
        ),
        in_specs=[vmem] * 6,
        out_specs=(vmem, vmem),
        cost_estimate=pl.CostEstimate(flops=tab.size * 8, bytes_accessed=4 << 20, transcendentals=0),
        compiler_params=pltpu.CompilerParams(vmem_limit_bytes=12 << 20),
        name="update",
    )(*ring_parts, acc.reshape(tables * subs, rows), tab)
    return out.reshape(acc.shape), new


def device_step(
    features, cotangent, cross_in, cross_out, bias, dest_shard, quot_row, rem_row,
    quot_slab, quot_accum, rem_table, rem_accum,
):
    samples = features.shape[0]
    tables = quot_slab.shape[0]
    width = quot_slab.shape[2]
    rem_rows = rem_table.shape[1]
    rows = NZ * NY
    cap = CAP
    ci, zi, yi = lax.axis_index("c"), lax.axis_index("z"), lax.axis_index("y")

    shard = dest_shard[:, :, 0]
    far_z = (shard // NY - zi) & (NZ - 1)
    far_y = (shard % NY - yi) & (NY - 1)
    target = jnp.where(ci == 0, far_z * NY + far_y, far_y * NZ + far_z)
    onehot = target[:, :, None] == jnp.arange(rows, dtype=jnp.int32)[None, None, :]
    lower = (
        jnp.arange(samples, dtype=jnp.int32)[:, None]
        >= jnp.arange(samples, dtype=jnp.int32)[None, :]
    ).astype(bf)
    running = jnp.einsum("ij,tjn->tin", lower, onehot.astype(bf), preferred_element_type=f32)
    slot_index = jnp.sum(jnp.where(onehot, running, 0.0), axis=2).astype(jnp.int32) - 1
    position = target * cap + slot_index
    digits = digit_lanes(quot_row, rem_row, width)

    position = position.reshape(tables, 1, samples)
    pieces, (position, digits) = rank_sums(
        features, cotangent, cross_in, cross_out, (position, digits)
    )
    xi = lax.axis_index("x")
    half = tables // 2
    dense = [
        pltpu.with_memory_space_constraint(a, pltpu.HBM)
        for a in (cotangent, cross_out, cross_in)
    ]
    rank = join(jnp.stack([ci, xi]).astype(jnp.int32), pieces)
    sends = []
    for first in (0, half):
        sends.append(
            pooled_dispatch(
                first, half, rank, *dense, bias.reshape(1, -1), position, digits,
                rows, cap, width,
            )
        )
    got_low, got_high = swap_rows(*sends)
    (slab,) = stage(quot_slab)
    along_z = ci == 0
    at_one = jnp.where(along_z, zi, yi)
    at_two = jnp.where(along_z, yi, zi)
    where = jnp.stack([ci, at_one, at_one]).astype(jnp.int32)
    half = tables // 2
    low = rem_parts(0, half, where, got_low, slab, rem_rows)
    high = rem_parts(half, half, where, got_high, slab, rem_rows)

    one_low, one_high = ring_scatter(low, high, False)
    ring_low, ring_high = ring_gather(one_low.astype(bf), one_high.astype(bf), True)
    share = rem_rows // rows
    view = (tables, NZ, NY, share)

    def quarter(a):
        a = a.reshape(view + a.shape[2:])
        return jnp.where(
            along_z,
            lax.dynamic_index_in_dim(a, zi, 1, keepdims=False),
            lax.dynamic_index_in_dim(a, yi, 2, keepdims=False),
        )

    acc_in, tab_in = quarter(rem_accum), quarter(rem_table)
    acc_low, new_low = update(ring_low, acc_in[:half], tab_in[:half])
    acc_high, new_high = update(ring_high, acc_in[half:], tab_in[half:])
    acc = jnp.concatenate([acc_low, acc_high], axis=0)
    rem_acc_out = lax.dynamic_index_in_dim(acc, at_two, 1, keepdims=False)
    all_low, all_high = ring_gather(new_low, new_high, False)
    shape = (tables, NZ, NY, share, width)
    near = [(all_low[k], all_high[k]) for k in (0, 1, 3)]
    rem_out = place((0, 1, 3), where, near, shape)
    rem_out = place((2,), where, [(all_low[2], all_high[2])], shape, rem_out)
    rem_out = rem_out.reshape(tables, rem_rows, width)

    quot_out, acc_low = quot_update(
        0, half, got_low, rem_table, quot_slab, quot_accum
    )
    quot_out, acc_high = quot_update(
        half, half, got_high, rem_table, quot_slab, quot_accum, quot_out
    )
    quot_acc_out = jnp.concatenate([acc_low[:half], acc_high[:half]], axis=0)
    return (quot_out, quot_acc_out, rem_out, rem_acc_out)


def solution(mesh):
    fine = Mesh(mesh.devices.reshape(NX, NC, NZ, NY), ("x", "c", "z", "y"))
    T, R = ("x", "c"), ("z", "y")
    return jax.shard_map(
        device_step,
        mesh=fine,
        in_specs=(
            P(R, T), P(R, T), P(T, None), P(T, None), P(T), P(T, R, None), P(T, R), P(T, R),
            P(T, R, None), P(T, R), P(T, None, None), P(T, None),
        ),
        out_specs=(P(T, R, None), P(T, R), P(T, None, None), P(T, R)),
        check_vma=False,
    )
```
